32 devices in a mesh: seq: 8 (over y, x, core), mp: 4 (over z).
Axes of the slice: x: 2, y: 2, z: 4, core: 2. Of those that a mesh axis runs over, the one named last changes fastest.
Arguments:
- latents: bfloat16 [4096, 5120], P('seq')
- modulation: float32 [6, 2, 5120], replicated, may hold values from -3 to 3
- w_qkv: bfloat16 [5120, 3, 2560], P(None, None, 'mp')
- qk_gains: float32 [2, 2560], P(None, 'mp'), may hold values from 0.5 to 4, as said below
- frame_counts: int32 [6], replicated, may hold values from 1 to 9, 16 in all
Outputs:
- attended: bfloat16 [4096, 2560], P('seq', 'mp')
The draws below stay inside these ranges and needn't reach their ends.
Inputs may be any that keep to these rules, and one draw needn't show every extreme that they name: `frame_counts`: they sum to 16, and the largest is exactly 9. `qk_gains`: positive gains.
All inputs are finite; a program needn't handle non-finite values.
Results may differ from the reference program's by a relative error of at most 0.0068.
Values may be sent and summed in bfloat16 or wider, within the bound.
A program may use at most 256 MiB of HBM per device.

```python
import math
import jax
import jax.numpy as jnp
import numpy as np
from jax import lax

D = 5120
HD = 128
GRID_W = 16
NSEG = 6
HEADS = 20
FRAME_TOK = 256
TOKENS = 4096
FRAMES = 16
SEG_FRAMES = 9


def draw_latents(key, part):
    keys = jax.random.split(key, 3)
    row_scale = jnp.exp(jax.random.uniform(keys[1], (TOKENS, 1), jnp.float32, 0.0, math.log(10.0)))
    col_scale = jnp.exp(jax.random.uniform(keys[2], (1, D), jnp.float32, 0.0, math.log(10.0)))
    base = jax.random.normal(keys[0], (TOKENS, D), jnp.float32)
    return (base * row_scale * col_scale).astype(jnp.bfloat16)


def draw_w_qkv(key, part):
    keys = jax.random.split(key, 2)
    width_all = HEADS * HD
    head_frac = (jnp.arange(width_all) // HD).astype(jnp.float32) / max(HEADS - 1, 1)
    col_scale = jnp.exp(jax.random.uniform(keys[1], (width_all,), jnp.float32, 0.0, math.log(10.0)))
    base = jax.random.normal(keys[0], (D, 3, width_all), jnp.float32) * D ** (-0.5)
    ramp = 3.0 ** (0.5 * head_frac)
    query_part = base[:, 0] * col_scale * ramp
    key_part = base[:, 1] * col_scale * ramp
    return jnp.stack([query_part, key_part, base[:, 2]], axis=1).astype(jnp.bfloat16)


def draw_qk_gains(key, part):
    return jnp.exp(jax.random.uniform(key, (2, HEADS * HD), jnp.float32, math.log(0.5), math.log(2.0)))


def length_profile(amount, total, most, skew):
    portions = [(1 << 20) // math.isqrt(grade ** skew) + 1 for grade in range(2, amount + 1)]
    spare, counts = total - most - (amount - 1), [1] * (amount - 1)
    while spare > 0:
        free = [i for i in range(amount - 1) if counts[i] < most]
        mass, budget = sum([portions[i] for i in free]), spare
        for i in free:
            extra = min(most - counts[i], max(1, budget * portions[i] // mass), spare)
            counts[i] = counts[i] + extra
            spare = spare - extra
    return np.array([most] + counts)


def ragged(stream_key, amount, total, reach, skew):
    if amount == 2:
        one = jax.random.randint(stream_key, (), max(1, total - reach), min(reach, total - 1) + 1)
        return jnp.stack([one, total - one])
    tallies = jnp.asarray(length_profile(amount, total, reach, skew), jnp.int32)
    pairs = (amount - 1) // 2
    donor, receiver = tallies[1:1 + 2 * pairs:2], tallies[2:2 + 2 * pairs:2]
    margin = jnp.minimum(donor - 1, reach - receiver)
    moved = jax.random.randint(jax.random.fold_in(stream_key, 1), (pairs,), 0, 1 << 20) % (margin + 1)
    tallies = tallies.at[1:1 + 2 * pairs:2].set(donor - moved).at[2:2 + 2 * pairs:2].set(receiver + moved)
    return tallies[jax.random.permutation(jax.random.fold_in(stream_key, 2), amount)]


def bell_draw(key, shape, scale, most, kind=jnp.bfloat16):
    values = scale * jax.random.normal(key, shape, jnp.float32)
    return jnp.clip(values, min=-most, max=most).astype(kind)


def setup_inputs(seed: int = 0) -> dict:
    key_list = jax.random.split(jax.random.key(seed), 6)
    return {
        "latents": draw_latents(jax.random.fold_in(key_list[5], 71), 0),
        "modulation": bell_draw(key_list[1], (NSEG, 2, D), 0.5, 3.0, jnp.float32),
        "w_qkv": draw_w_qkv(jax.random.fold_in(key_list[5], 71), 0),
        "qk_gains": draw_qk_gains(jax.random.fold_in(key_list[5], 71), 0),
        "frame_counts": ragged(key_list[4], NSEG, FRAMES, SEG_FRAMES, 2).astype(jnp.int32),
    }


def token_layout(indices, frame_counts):
    frames = indices // FRAME_TOK
    ends = jnp.cumsum(frame_counts).astype(jnp.int32)
    segment = lax.optimization_barrier(jnp.sum((frames[:, None] >= ends[None, :]).astype(jnp.int32), axis=1)).astype(jnp.int32)
    starts = (ends - frame_counts).astype(jnp.int32)
    chosen = segment[:, None] == jnp.arange(NSEG, dtype=jnp.int32)[None, :]
    first_frame = lax.optimization_barrier(jnp.sum(jnp.where(chosen, starts[None, :], 0), axis=1)).astype(jnp.int32)
    return (segment, frames - first_frame, indices % FRAME_TOK // GRID_W, indices % GRID_W)

def rope_tables(frame_pos, row_pos, col_pos, head_dim):
    sixth_part = head_dim // 6
    frame_dim = head_dim - 4 * sixth_part
    side_dim = 2 * sixth_part
    frame_freq = 10000.0 ** (-np.arange(0, frame_dim, 2) / frame_dim)
    side_freq = 10000.0 ** (-np.arange(0, side_dim, 2) / side_dim)
    empty_frame = np.zeros(frame_dim // 2)
    empty_side = np.zeros(sixth_part)
    along_frame = jnp.asarray(np.concatenate([frame_freq, empty_side, empty_side]), jnp.float32)
    along_rows = jnp.asarray(np.concatenate([empty_frame, side_freq, empty_side]), jnp.float32)
    along_cols = jnp.asarray(np.concatenate([empty_frame, empty_side, side_freq]), jnp.float32)
    angles = frame_pos.astype(jnp.float32)[:, None] * along_frame[None, :] + row_pos.astype(jnp.float32)[:, None] * along_rows[None, :] + col_pos.astype(jnp.float32)[:, None] * along_cols[None, :]
    return (jnp.cos(angles), jnp.sin(angles))

def apply_rotary(values, cosine, sine):
    shaped = values.reshape(values.shape[0], values.shape[1], -1, 2)
    first_part = shaped[..., 0]
    second_part = shaped[..., 1]
    cos_wide = cosine[:, None, :]
    sin_wide = sine[:, None, :]
    turned = jnp.stack([first_part * cos_wide - second_part * sin_wide, first_part * sin_wide + second_part * cos_wide], axis=-1)
    return turned.reshape(values.shape)

def modulate(latents, modulation, segment):
    floats = latents.astype(jnp.float32)
    average = lax.optimization_barrier(jnp.mean(floats, axis=1, keepdims=True))
    centred = floats - average
    variance = lax.optimization_barrier(jnp.mean(centred * centred, axis=1, keepdims=True))
    normed = centred * lax.rsqrt(variance + 1e-06)
    chosen = (segment[:, None] == jnp.arange(NSEG, dtype=jnp.int32)[None, :]).astype(jnp.float32)
    shifts = jnp.dot(chosen, modulation[:, 0, :], precision=lax.Precision.HIGHEST)
    scales = jnp.dot(chosen, modulation[:, 1, :], precision=lax.Precision.HIGHEST)
    return (normed * (1.0 + scales) + shifts).astype(jnp.bfloat16)

def reference(latents, modulation, w_qkv, qk_gains, frame_counts):
    tokens = latents.shape[0]
    indices = jnp.arange(tokens, dtype=jnp.int32)
    segment, frame_pos, row_pos, col_pos = token_layout(indices, frame_counts)
    modulated = modulate(latents, modulation, segment)
    width_all = HEADS * HD
    projected = jnp.dot(modulated, w_qkv.reshape(D, 3 * width_all), preferred_element_type=jnp.float32)
    q_raw = projected[:, :width_all]
    k_raw = projected[:, width_all:2 * width_all]
    values = projected[:, 2 * width_all:].astype(jnp.bfloat16)
    q_norm = q_raw * lax.rsqrt(lax.optimization_barrier(jnp.mean(q_raw * q_raw, axis=1, keepdims=True)) + 1e-06) * qk_gains[0][None, :]
    k_norm = k_raw * lax.rsqrt(lax.optimization_barrier(jnp.mean(k_raw * k_raw, axis=1, keepdims=True)) + 1e-06) * qk_gains[1][None, :]
    cosine, sine = rope_tables(frame_pos, row_pos, col_pos, HD)
    queries = apply_rotary(q_norm.reshape(tokens, HEADS, HD), cosine, sine).astype(jnp.bfloat16)
    keys = apply_rotary(k_norm.reshape(tokens, HEADS, HD), cosine, sine).astype(jnp.bfloat16)
    key_floats = keys.astype(jnp.float32)
    value_floats = values.astype(jnp.float32).reshape(tokens, HEADS, HD)
    block_rows = math.gcd(tokens, 256)
    scale_factor = 1.0 / math.sqrt(HD)

    def one_block(position):
        query_block = lax.dynamic_slice_in_dim(queries, position * block_rows, block_rows, 0).astype(jnp.float32)
        query_seg = lax.dynamic_slice_in_dim(segment, position * block_rows, block_rows, 0)
        scores = jnp.einsum('qhd,khd->hqk', query_block, key_floats, precision=lax.Precision.HIGHEST) * scale_factor
        allowed = query_seg[None, :, None] == segment[None, None, :]
        row_max = lax.optimization_barrier(jnp.max(jnp.where(allowed, scores, -1e+30), axis=2, keepdims=True))
        weights = jnp.where(allowed, jnp.exp(scores - row_max), 0.0)
        totals = lax.optimization_barrier(jnp.sum(weights, axis=2))
        rounded = lax.optimization_barrier(weights.astype(jnp.bfloat16))
        summed = jnp.einsum('hqk,khd->qhd', rounded.astype(jnp.float32), value_floats, precision=lax.Precision.HIGHEST)
        result = summed / jnp.transpose(totals)[:, :, None]
        return result.astype(jnp.bfloat16).reshape(block_rows, width_all)
    blocks = lax.map(one_block, jnp.arange(tokens // block_rows, dtype=jnp.int32))
    return blocks.reshape(tokens, width_all)
```

```python
import math

import jax
import jax.numpy as jnp
import numpy as np
from jax import lax
from jax.experimental import pallas as pl
from jax.experimental.pallas import tpu as pltpu
from jax.sharding import PartitionSpec as P

HD = 128
GRID_W = 16
NSEG = 6
FRAME_TOK = 256


mask_floor = -1e30


def token_layout(indices, frame_counts):
    frames = indices // FRAME_TOK
    lower = np.tril(np.ones((NSEG, NSEG), np.int32))
    ends = jnp.sum(frame_counts[None, :] * lower, axis=1)
    segment = jnp.sum((frames[:, None] >= ends[None, :]).astype(jnp.int32), axis=1)
    starts = ends - frame_counts
    chosen = segment[:, None] == jnp.arange(NSEG, dtype=jnp.int32)[None, :]
    first_frame = jnp.sum(jnp.where(chosen, starts[None, :], 0), axis=1)
    return (segment, frames - first_frame, indices % FRAME_TOK // GRID_W, indices % GRID_W)


def rope_tables(frame_pos, row_pos, col_pos, head_dim):
    sixth_part = head_dim // 6
    frame_dim = head_dim - 4 * sixth_part
    side_dim = 2 * sixth_part
    frame_freq = 10000.0 ** (-np.arange(0, frame_dim, 2) / frame_dim)
    side_freq = 10000.0 ** (-np.arange(0, side_dim, 2) / side_dim)
    empty_frame = np.zeros(frame_dim // 2)
    empty_side = np.zeros(sixth_part)
    along_frame = jnp.asarray(np.concatenate([frame_freq, empty_side, empty_side]), jnp.float32)
    along_rows = jnp.asarray(np.concatenate([empty_frame, side_freq, empty_side]), jnp.float32)
    along_cols = jnp.asarray(np.concatenate([empty_frame, empty_side, side_freq]), jnp.float32)
    angles = (
        frame_pos.astype(jnp.float32)[:, None] * along_frame[None, :]
        + row_pos.astype(jnp.float32)[:, None] * along_rows[None, :]
        + col_pos.astype(jnp.float32)[:, None] * along_cols[None, :]
    )
    return (jnp.cos(angles), jnp.sin(angles))


def apply_rotary(values, cosine, sine):
    shaped = values.reshape(values.shape[0], values.shape[1], -1, 2)
    first_part = shaped[..., 0]
    second_part = shaped[..., 1]
    cos_wide = cosine[:, None, :]
    sin_wide = sine[:, None, :]
    turned = jnp.stack(
        [
            first_part * cos_wide - second_part * sin_wide,
            first_part * sin_wide + second_part * cos_wide,
        ],
        axis=-1,
    )
    return turned.reshape(values.shape)


def modulate(latents, modulation, segment):
    floats = latents.astype(jnp.float32)
    average = jnp.mean(floats, axis=1, keepdims=True)
    centred = floats - average
    variance = jnp.mean(centred * centred, axis=1, keepdims=True)
    normed = centred * lax.rsqrt(variance + 1e-06)
    chosen = (segment[:, None] == jnp.arange(NSEG, dtype=jnp.int32)[None, :]).astype(jnp.float32)
    shifts = jnp.dot(chosen, modulation[:, 0, :], precision=lax.Precision.HIGHEST)
    scales = jnp.dot(chosen, modulation[:, 1, :], precision=lax.Precision.HIGHEST)
    return (normed * (1.0 + scales) + shifts).astype(jnp.bfloat16)


def attend_block(state, key_block, key_segs, queries, query_seg):
    maxima, totals, accum = state
    heads = queries.shape[1]
    keys_three = key_block[0].reshape(-1, heads, HD)
    values_three = key_block[1].reshape(-1, heads, HD)
    scores = jnp.einsum("qhd,khd->hqk", queries, keys_three, preferred_element_type=jnp.float32) * (
        1.0 / math.sqrt(HD)
    )
    allowed = query_seg[None, :, None] == key_segs[None, None, :]
    newest = jnp.maximum(maxima, jnp.max(jnp.where(allowed, scores, mask_floor), axis=2))
    weights = jnp.where(allowed, jnp.exp(scores - newest[:, :, None]), 0.0)
    factor = jnp.exp(maxima - newest)
    totals = totals * factor + jnp.sum(weights, axis=2)
    product = jnp.einsum(
        "hqk,khd->qhd",
        weights.astype(jnp.bfloat16),
        values_three,
        preferred_element_type=jnp.float32,
    )
    accum = accum * jnp.transpose(factor)[:, :, None] + product
    return (newest, totals, accum)


def attend_piece(state, pieces, key_seg, queries, query_seg):
    count_rows = pieces.shape[1]
    span_rows = math.gcd(count_rows, 512)

    def guarded(carried, key_block, key_segs):
        touches = jnp.logical_and(
            jnp.max(key_segs) >= query_seg[0],
            jnp.min(jnp.where(key_segs >= 0, key_segs, NSEG)) <= query_seg[-1],
        )
        return lax.cond(
            touches,
            lambda inner: attend_block(inner, key_block, key_segs, queries, query_seg),
            lambda inner: inner,
            carried,
        )

    def advance(position, carried):
        key_block = lax.dynamic_slice_in_dim(pieces, position * span_rows, span_rows, 1)
        key_segs = lax.dynamic_slice_in_dim(key_seg, position * span_rows, span_rows, 0)
        return guarded(carried, key_block, key_segs)

    return lax.fori_loop(0, count_rows // span_rows, advance, state)


def body(latents, modulation, w_qkv, qk_gains, frame_counts):
    rows = latents.shape[0]
    model_width = latents.shape[1]
    width_dev = w_qkv.shape[2]
    heads = width_dev // HD
    me_seq = lax.axis_index("seq")
    row_ids = jnp.arange(rows, dtype=jnp.int32)
    indices = me_seq * rows + row_ids
    segment, frame_pos, row_pos, col_pos = token_layout(indices, frame_counts)
    modulated = modulate(latents, modulation, segment)
    projected = jnp.dot(
        modulated, w_qkv.reshape(model_width, 3 * width_dev), preferred_element_type=jnp.float32
    )
    q_raw = projected[:, :width_dev]
    k_raw = projected[:, width_dev : 2 * width_dev]
    values = projected[:, 2 * width_dev :].astype(jnp.bfloat16)
    partial_sums = jnp.stack([jnp.sum(q_raw * q_raw, axis=1), jnp.sum(k_raw * k_raw, axis=1)])
    squares = lax.psum(partial_sums, "mp")
    channels = width_dev * lax.axis_size("mp")
    q_norm = q_raw * lax.rsqrt(squares[0] / channels + 1e-06)[:, None] * qk_gains[0][None, :]
    k_norm = k_raw * lax.rsqrt(squares[1] / channels + 1e-06)[:, None] * qk_gains[1][None, :]
    cosine, sine = rope_tables(frame_pos, row_pos, col_pos, HD)
    queries = apply_rotary(q_norm.reshape(rows, heads, HD), cosine, sine).astype(jnp.bfloat16)
    keys = apply_rotary(k_norm.reshape(rows, heads, HD), cosine, sine).astype(jnp.bfloat16)
    stacked = jnp.stack([keys.reshape(rows, width_dev), values])
    initial = (
        jnp.full((heads, rows), mask_floor, jnp.float32),
        jnp.zeros((heads, rows), jnp.float32),
        jnp.zeros((rows, heads, HD), jnp.float32),
    )
    piece = lax.all_gather(stacked, "seq", axis=1, tiled=True)
    key_index = jnp.arange(piece.shape[1], dtype=jnp.int32)
    key_seg = token_layout(key_index, frame_counts)[0]
    state = attend_piece(initial, piece, key_seg, queries, segment)
    maxima, totals, accum = state
    result = accum / jnp.transpose(totals)[:, :, None]
    return result.astype(jnp.bfloat16).reshape(rows, width_dev)


SLOTS = 8
CHUNKS = 4


def rotary_constants(positions):
    sixth_part = HD // 6
    frame_dim = HD - 4 * sixth_part
    side_dim = 2 * sixth_part
    frame_freq = 10000.0 ** (-np.arange(0, frame_dim, 2) / frame_dim)
    side_freq = 10000.0 ** (-np.arange(0, side_dim, 2) / side_dim)
    token = np.arange(FRAME_TOK)
    angles = np.zeros((FRAME_TOK, HD // 2))
    angles[:, frame_dim // 2 : frame_dim // 2 + sixth_part] = (token // GRID_W)[:, None] * side_freq
    angles[:, frame_dim // 2 + sixth_part :] = (token % GRID_W)[:, None] * side_freq
    wide = np.repeat(angles, 2, axis=1)
    lane = np.arange(HD)
    even = (lane % 2 == 0)[None, :]
    side = (lane >= frame_dim)[None, :]
    tables = np.stack(
        [
            np.where(side, np.cos(wide), 0.0),
            np.where(side & even, -np.sin(wide), 0.0),
            np.where(side & ~even, np.sin(wide), 0.0),
        ]
    )
    turns = np.arange(positions)[:, None] * np.repeat(frame_freq, 2)
    turns = np.pad(turns, ((0, 0), (0, HD - frame_dim)))
    rows = np.stack(
        [
            np.where(side, 0.0, np.cos(turns)),
            np.where(even, -np.sin(turns), 0.0),
            np.where(even, 0.0, np.sin(turns)),
        ],
        axis=1,
    )
    return tables.astype(np.float32), rows.astype(np.float32)


def fused_kernel(
    counts_ref, x_hbm, w_hbm, mod_ref, gain_ref, side_ref, table_ref, out_ref,
    bias_ref, frame_ref, xbuf, ybuf, wbuf, kvg, qbuf, acc, rows_mod, squares, rkeys, maxima, totals, accum,
    xsem, wsem, fsem, ssem, rsem, qs_sem, qr_sem, ks_sem, kr_sem,
):
    rows, width = xbuf.shape
    heads = qbuf.shape[1] // HD
    chunk = width // CHUNKS
    me = lax.axis_index("seq")
    me_mp = lax.axis_index("mp")
    n_mp = squares.shape[1]
    channels = heads * HD * n_mp
    frames = rows // FRAME_TOK

    def peer(rel):
        target = me
        for bit in (1, 2, 4):
            if rel & bit:
                target = target + bit - 2 * bit * (me // bit % 2)
        return {"seq": target}

    def peer_mp(rel):
        return {"mp": (me_mp + rel) % n_mp}

    def x_copy(f):
        span = pl.ds(f * FRAME_TOK, FRAME_TOK)
        return pltpu.make_async_copy(x_hbm.at[span], xbuf.at[span], xsem.at[f])

    def w_copy(which, j):
        span = pl.ds(pl.multiple_of(j * chunk, chunk), chunk)
        return pltpu.make_async_copy(
            w_hbm.at[which, span], wbuf.at[which, span], wsem.at[which, j]
        )

    for f in range(frames):
        x_copy(f).start()
    for which in (1, 2, 0):
        for j in range(CHUNKS):
            w_copy(which, j).start()

    barrier = pltpu.get_barrier_semaphore()
    for rel in range(1, SLOTS):
        pl.semaphore_signal(barrier, inc=1, device_id=peer(rel), device_id_type=pl.DeviceIdType.MESH)
    for rel in range(1, n_mp):
        pl.semaphore_signal(barrier, inc=1, device_id=peer_mp(rel), device_id_type=pl.DeviceIdType.MESH)

    ends, starts = [], []
    for s in range(NSEG):
        starts.append(ends[-1] if s else jnp.int32(0))
        ends.append(starts[-1] + counts_ref[s])

    def segment_of(frame):
        return sum(jnp.where(frame >= end, 1, 0) for end in ends)

    own_seg = [segment_of(me * frames + f) for f in range(frames)]
    for rel in range(SLOTS):
        for g in range(frames):
            key_seg = segment_of(peer(rel)["seq"] * frames + g)
            for f in range(frames):
                bias_ref[f, rel * frames + g] = jnp.where(own_seg[f] == key_seg, 0.0, mask_floor)

    for f in range(frames):
        chosen_start = sum(jnp.where(own_seg[f] == s, starts[s], 0) for s in range(NSEG))
        frame_ref[f] = table_ref[jnp.clip(me * frames + f - chosen_start, 0, table_ref.shape[0] - 1)]
        pair = mod_ref[jnp.minimum(own_seg[f], NSEG - 1)]
        rows_mod[2 * f] = jnp.broadcast_to(pair[0:1, :], (8, width))
        rows_mod[2 * f + 1] = jnp.broadcast_to(1.0 + pair[1:2, :], (8, width))

    def norm_frame(f):
        x_copy(f).wait()

        block, lanes = 128, 128
        groups = width // lanes
        for i in range(FRAME_TOK // block):
            span = slice(f * FRAME_TOK + i * block, f * FRAME_TOK + (i + 1) * block)

            def load(k):
                return xbuf[span, k * lanes : (k + 1) * lanes].astype(jnp.float32)

            total = load(0)
            for k in range(1, groups):
                total = total + load(k)
            average = jnp.sum(total, axis=1, keepdims=True) * (1.0 / width)
            power = jnp.zeros((block, lanes), jnp.float32)
            for k in range(groups):
                centred = load(k) - average
                power = power + centred * centred
            variance = jnp.sum(power, axis=1, keepdims=True) * (1.0 / width)
            inverse = lax.rsqrt(variance + 1e-06)
            for k in range(groups):
                cols = slice(k * lanes, (k + 1) * lanes)
                normed = ((load(k) - average) * inverse).reshape(block // 8, 8, lanes)
                scaled = normed * rows_mod[2 * f + 1, :, cols] + rows_mod[2 * f, :, cols]
                ybuf[span, cols] = scaled.reshape(block, lanes).astype(jnp.bfloat16)

    def project(which, first, last, wait):
        if wait:
            for j in range(CHUNKS):
                w_copy(which, j).wait()
        acc[first:last, :] = jnp.dot(ybuf[first:last, :], wbuf[which], preferred_element_type=jnp.float32)

    def row_squares(kind):
        total = jnp.zeros((rows, HD), jnp.float32)
        for h in range(heads):
            piece = acc[:, h * HD : (h + 1) * HD]
            total = total + piece * piece
        squares[kind, 0] = lax.dot_general(
            jnp.ones((8, HD), jnp.float32), total, (((1,), (1,)), ((), ())),
            precision=lax.Precision.HIGHEST, preferred_element_type=jnp.float32,
        )

    def rotate(kind, f, h):
        span = slice(f * FRAME_TOK, (f + 1) * FRAME_TOK)
        lanes = slice(h * HD, (h + 1) * HD)
        value = acc[span, lanes] * gain_ref[kind : kind + 1, lanes]
        cosine = side_ref[0] + frame_ref[f, 0:1, :]
        below = side_ref[1] + frame_ref[f, 1:2, :]
        above = side_ref[2] + frame_ref[f, 2:3, :]
        return value * cosine + pltpu.roll(value, HD - 1, 1) * below + pltpu.roll(value, 1, 1) * above

    key_sends = [(f, rel) for f in range(frames) for rel in (2, 4, 1)]
    first_sends = [(0, 1, 4, 4), (0, 1, 2, 2), (0, 1, 1, 1)]
    later_sends = [
        (2, 0, 4, 6), (4, 1, 2, 6),
        (2, 0, 1, 3), (2, 1, 1, 3), (4, 0, 1, 5), (4, 1, 1, 5),
        (6, 0, 1, 7), (6, 1, 1, 7),
    ]
    sends = first_sends + later_sends

    def send(entry):
        source, part, rel, landing = entry
        return pltpu.make_async_remote_copy(
            src_ref=kvg.at[source, part], dst_ref=kvg.at[landing, part],
            send_sem=ssem.at[sends.index(entry)], recv_sem=rsem.at[landing, part],
            device_id=peer(rel), device_id_type=pl.DeviceIdType.MESH,
        )

    def send_keys(f, rel):
        span = pl.ds(f * FRAME_TOK, FRAME_TOK)
        return pltpu.make_async_remote_copy(
            src_ref=kvg.at[0, 0, span], dst_ref=kvg.at[rel, 0, span],
            send_sem=fsem.at[key_sends.index((f, rel))], recv_sem=rsem.at[rel, 0],
            device_id=peer(rel), device_id_type=pl.DeviceIdType.MESH,
        )

    def arrived(slot, part):
        pltpu.make_async_copy(kvg.at[slot, part], kvg.at[slot, part], rsem.at[slot, part]).wait()

    def send_squares(kind, rel):
        return pltpu.make_async_remote_copy(
            src_ref=squares.at[kind, 0], dst_ref=squares.at[kind, rel],
            send_sem=qs_sem.at[kind, rel], recv_sem=qr_sem.at[kind, rel],
            device_id=peer_mp(rel), device_id_type=pl.DeviceIdType.MESH,
        )

    def send_rkeys(rel):
        return pltpu.make_async_remote_copy(
            src_ref=rkeys.at[0], dst_ref=rkeys.at[rel],
            send_sem=ks_sem.at[rel], recv_sem=kr_sem.at[rel],
            device_id=peer(rel), device_id_type=pl.DeviceIdType.MESH,
        )

    def inverse_rms(kind):
        total = squares[kind, 0]
        for rel in range(1, n_mp):
            send_squares(kind, rel).wait_recv()
            total = total + squares[kind, rel]
        return lax.rsqrt(total * (1.0 / channels) + 1e-06)

    for f in range(frames):
        norm_frame(f)
        project(1, f * FRAME_TOK, (f + 1) * FRAME_TOK, f == 0)
        for h in range(heads):
            kvg[0, 0, f * FRAME_TOK : (f + 1) * FRAME_TOK, h * HD : (h + 1) * HD] = rotate(1, f, h).astype(jnp.bfloat16)
        if f == 0:
            pl.semaphore_wait(barrier, SLOTS - 1 + n_mp - 1)
        for rel in (2, 4, 1):
            send_keys(f, rel).start()
    row_squares(1)
    for rel in range(1, n_mp):
        send_squares(1, rel).start()

    project(2, 0, rows, True)
    kvg[0, 1] = acc[...].astype(jnp.bfloat16)
    for entry in first_sends:
        send(entry).start()
    rkeys[0] = inverse_rms(1) * (math.log2(math.e) / math.sqrt(HD))
    for rel in range(1, SLOTS):
        send_rkeys(rel).start()

    project(0, 0, rows, True)
    row_squares(0)
    for rel in range(1, n_mp):
        send_squares(0, rel).start()
    for f in range(frames):
        for h in range(heads):
            accum[f * FRAME_TOK : (f + 1) * FRAME_TOK, h * HD : (h + 1) * HD] = rotate(0, f, h)

    arrived(2, 0)
    send(later_sends[0]).start()
    send(later_sends[2]).start()
    arrived(4, 1)
    send(later_sends[1]).start()
    send(later_sends[5]).start()
    arrived(2, 1)
    send(later_sends[3]).start()
    arrived(4, 0)
    send(later_sends[4]).start()

    rquery = inverse_rms(0)
    column = jnp.transpose(jnp.broadcast_to(rquery[0:1, :], (HD, rows)))
    for h in range(heads):
        lanes = slice(h * HD, (h + 1) * HD)
        qbuf[:, lanes] = (accum[:, lanes] * column).astype(jnp.bfloat16)

    maxima[...] = jnp.full(maxima.shape, mask_floor, jnp.float32)
    totals[...] = jnp.zeros(totals.shape, jnp.float32)
    accum[...] = jnp.zeros(accum.shape, jnp.float32)

    def wait_slot(slot):
        arrived(slot, 0)
        arrived(slot, 1)

    def attend_slot(slot, carry):
        @pl.when(slot > 0)
        def _():
            pltpu.make_async_copy(rkeys.at[slot], rkeys.at[slot], kr_sem.at[slot]).wait()

        @pl.when(jnp.logical_or(slot == 1, jnp.logical_or(slot == 3, slot == 5)))
        def _():
            wait_slot(slot)

        @pl.when(slot == 7)
        def _():
            wait_slot(slot)

        @pl.when(slot == 6)
        def _():
            arrived(6, 0)
            send(later_sends[6]).start()
            arrived(6, 1)
            send(later_sends[7]).start()

        def attend_frame(f, inner):
            span = pl.ds(pl.multiple_of(f * FRAME_TOK, FRAME_TOK), FRAME_TOK)
            lane = lax.broadcasted_iota(jnp.int32, (1, rows), 1)
            shift = jnp.full((1, rows), bias_ref[f, slot * frames], jnp.float32)
            for g in range(1, frames):
                shift = jnp.where(lane >= g * FRAME_TOK, bias_ref[f, slot * frames + g], shift)
            scale = rkeys[slot, 0:1, :]

            def score(h):
                lanes = slice(h * HD, (h + 1) * HD)
                return lax.dot_general(
                    qbuf[span, lanes], kvg[slot, 0, :, lanes], (((1,), (1,)), ((), ())),
                    preferred_element_type=jnp.float32,
                )

            ones = jnp.ones((rows, HD), jnp.bfloat16)
            ahead = score(0)
            for h in range(heads):
                lanes = slice(h * HD, (h + 1) * HD)
                scores = ahead * scale + shift
                if h + 1 < heads:
                    ahead = score(h + 1)
                before = maxima[h, span, :]
                newest = jnp.maximum(before, jnp.max(scores, axis=1, keepdims=True))
                weights = jnp.exp2(scores - newest[:, 0:1]).astype(jnp.bfloat16)
                factor = jnp.exp2(before - newest)
                wide = jnp.concatenate([kvg[slot, 1, :, lanes], ones], axis=1)
                product = jnp.dot(weights, wide, preferred_element_type=jnp.float32)
                totals[h, span, :] = totals[h, span, :] * factor + product[:, HD:]
                accum[span, lanes] = accum[span, lanes] * factor + product[:, :HD]
                maxima[h, span, :] = newest
            return inner

        return lax.fori_loop(0, frames, attend_frame, carry)

    lax.fori_loop(0, SLOTS, attend_slot, 0)
    for h in range(heads):
        lanes = slice(h * HD, (h + 1) * HD)
        out_ref[:, lanes] = (accum[:, lanes] / totals[h]).astype(jnp.bfloat16)

    for f, rel in key_sends:
        send_keys(f, rel).wait_send()
    for entry in sends:
        send(entry).wait_send()
    for rel in range(1, n_mp):
        send_squares(0, rel).wait_send()
        send_squares(1, rel).wait_send()
    for rel in range(1, SLOTS):
        send_rkeys(rel).wait_send()


def fused_body(latents, modulation, w_qkv, qk_gains, frame_counts):
    rows, width = latents.shape
    width_dev = w_qkv.shape[2]
    heads = width_dev // HD
    frames = rows // FRAME_TOK
    n_mp = lax.axis_size("mp")
    side, table = rotary_constants(SLOTS * frames)
    weights = jnp.transpose(w_qkv, (1, 0, 2))
    vmem = pl.BlockSpec(memory_space=pltpu.VMEM)
    smem = pl.BlockSpec(memory_space=pltpu.SMEM)
    hbm = pl.BlockSpec(memory_space=pl.ANY)
    dma = pltpu.SemaphoreType.DMA
    flops = 2 * rows * width * 3 * width_dev + 4 * rows * rows * SLOTS * width_dev
    return pl.pallas_call(
        fused_kernel,
        out_shape=jax.ShapeDtypeStruct((rows, width_dev), jnp.bfloat16),
        in_specs=[smem, hbm, hbm, vmem, vmem, vmem, vmem],
        out_specs=vmem,
        scratch_shapes=[
            pltpu.SMEM((frames, SLOTS * frames), jnp.float32),
            pltpu.VMEM((frames, 3, HD), jnp.float32),
            pltpu.VMEM((rows, width), jnp.bfloat16),
            pltpu.VMEM((rows, width), jnp.bfloat16),
            pltpu.VMEM((3, width, width_dev), jnp.bfloat16),
            pltpu.VMEM((SLOTS, 2, rows, width_dev), jnp.bfloat16),
            pltpu.VMEM((rows, width_dev), jnp.bfloat16),
            pltpu.VMEM((rows, width_dev), jnp.float32),
            pltpu.VMEM((2 * frames, 8, width), jnp.float32),
            pltpu.VMEM((2, n_mp, 8, rows), jnp.float32),
            pltpu.VMEM((SLOTS, 8, rows), jnp.float32),
            pltpu.VMEM((heads, rows, HD), jnp.float32),
            pltpu.VMEM((heads, rows, HD), jnp.float32),
            pltpu.VMEM((rows, width_dev), jnp.float32),
            dma((frames,)),
            dma((3, CHUNKS)),
            dma((3 * frames,)),
            dma((11,)),
            dma((SLOTS, 2)),
            dma((2, n_mp)),
            dma((2, n_mp)),
            dma((SLOTS,)),
            dma((SLOTS,)),
        ],
        compiler_params=pltpu.CompilerParams(
            collective_id=0, has_side_effects=True, vmem_limit_bytes=60 * 1024 * 1024
        ),
        cost_estimate=pl.CostEstimate(flops=flops, bytes_accessed=30000000, transcendentals=12000000),
    )(frame_counts, latents, weights, modulation, qk_gains, side, table)


def solution(mesh):
    in_specs = (P("seq", None), P(), P(None, None, "mp"), P(None, "mp"), P())
    out_specs = P("seq", "mp")
    chosen = fused_body if mesh.shape["seq"] == SLOTS else body
    return jax.shard_map(chosen, mesh=mesh, in_specs=in_specs, out_specs=out_specs, check_vma=False)
```

```python
import math

import jax
import jax.numpy as jnp
import numpy as np
from jax import lax
from jax.experimental import pallas as pl
from jax.experimental.pallas import tpu as pltpu
from jax.sharding import PartitionSpec as P

HD = 128
GRID_W = 16
NSEG = 6
FRAME_TOK = 256


mask_floor = -1e30


def token_layout(indices, frame_counts):
    frames = indices // FRAME_TOK
    lower = np.tril(np.ones((NSEG, NSEG), np.int32))
    ends = jnp.sum(frame_counts[None, :] * lower, axis=1)
    segment = jnp.sum((frames[:, None] >= ends[None, :]).astype(jnp.int32), axis=1)
    starts = ends - frame_counts
    chosen = segment[:, None] == jnp.arange(NSEG, dtype=jnp.int32)[None, :]
    first_frame = jnp.sum(jnp.where(chosen, starts[None, :], 0), axis=1)
    return (segment, frames - first_frame, indices % FRAME_TOK // GRID_W, indices % GRID_W)


def rope_tables(frame_pos, row_pos, col_pos, head_dim):
    sixth_part = head_dim // 6
    frame_dim = head_dim - 4 * sixth_part
    side_dim = 2 * sixth_part
    frame_freq = 10000.0 ** (-np.arange(0, frame_dim, 2) / frame_dim)
    side_freq = 10000.0 ** (-np.arange(0, side_dim, 2) / side_dim)
    empty_frame = np.zeros(frame_dim // 2)
    empty_side = np.zeros(sixth_part)
    along_frame = jnp.asarray(np.concatenate([frame_freq, empty_side, empty_side]), jnp.float32)
    along_rows = jnp.asarray(np.concatenate([empty_frame, side_freq, empty_side]), jnp.float32)
    along_cols = jnp.asarray(np.concatenate([empty_frame, empty_side, side_freq]), jnp.float32)
    angles = (
        frame_pos.astype(jnp.float32)[:, None] * along_frame[None, :]
        + row_pos.astype(jnp.float32)[:, None] * along_rows[None, :]
        + col_pos.astype(jnp.float32)[:, None] * along_cols[None, :]
    )
    return (jnp.cos(angles), jnp.sin(angles))


def apply_rotary(values, cosine, sine):
    shaped = values.reshape(values.shape[0], values.shape[1], -1, 2)
    first_part = shaped[..., 0]
    second_part = shaped[..., 1]
    cos_wide = cosine[:, None, :]
    sin_wide = sine[:, None, :]
    turned = jnp.stack(
        [
            first_part * cos_wide - second_part * sin_wide,
            first_part * sin_wide + second_part * cos_wide,
        ],
        axis=-1,
    )
    return turned.reshape(values.shape)


def modulate(latents, modulation, segment):
    floats = latents.astype(jnp.float32)
    average = jnp.mean(floats, axis=1, keepdims=True)
    centred = floats - average
    variance = jnp.mean(centred * centred, axis=1, keepdims=True)
    normed = centred * lax.rsqrt(variance + 1e-06)
    chosen = (segment[:, None] == jnp.arange(NSEG, dtype=jnp.int32)[None, :]).astype(jnp.float32)
    shifts = jnp.dot(chosen, modulation[:, 0, :], precision=lax.Precision.HIGHEST)
    scales = jnp.dot(chosen, modulation[:, 1, :], precision=lax.Precision.HIGHEST)
    return (normed * (1.0 + scales) + shifts).astype(jnp.bfloat16)


def attend_block(state, key_block, key_segs, queries, query_seg):
    maxima, totals, accum = state
    heads = queries.shape[1]
    keys_three = key_block[0].reshape(-1, heads, HD)
    values_three = key_block[1].reshape(-1, heads, HD)
    scores = jnp.einsum("qhd,khd->hqk", queries, keys_three, preferred_element_type=jnp.float32) * (
        1.0 / math.sqrt(HD)
    )
    allowed = query_seg[None, :, None] == key_segs[None, None, :]
    newest = jnp.maximum(maxima, jnp.max(jnp.where(allowed, scores, mask_floor), axis=2))
    weights = jnp.where(allowed, jnp.exp(scores - newest[:, :, None]), 0.0)
    factor = jnp.exp(maxima - newest)
    totals = totals * factor + jnp.sum(weights, axis=2)
    product = jnp.einsum(
        "hqk,khd->qhd",
        weights.astype(jnp.bfloat16),
        values_three,
        preferred_element_type=jnp.float32,
    )
    accum = accum * jnp.transpose(factor)[:, :, None] + product
    return (newest, totals, accum)


def attend_piece(state, pieces, key_seg, queries, query_seg):
    count_rows = pieces.shape[1]
    span_rows = math.gcd(count_rows, 512)

    def guarded(carried, key_block, key_segs):
        touches = jnp.logical_and(
            jnp.max(key_segs) >= query_seg[0],
            jnp.min(jnp.where(key_segs >= 0, key_segs, NSEG)) <= query_seg[-1],
        )
        return lax.cond(
            touches,
            lambda inner: attend_block(inner, key_block, key_segs, queries, query_seg),
            lambda inner: inner,
            carried,
        )

    def advance(position, carried):
        key_block = lax.dynamic_slice_in_dim(pieces, position * span_rows, span_rows, 1)
        key_segs = lax.dynamic_slice_in_dim(key_seg, position * span_rows, span_rows, 0)
        return guarded(carried, key_block, key_segs)

    return lax.fori_loop(0, count_rows // span_rows, advance, state)


def body(latents, modulation, w_qkv, qk_gains, frame_counts):
    rows = latents.shape[0]
    model_width = latents.shape[1]
    width_dev = w_qkv.shape[2]
    heads = width_dev // HD
    me_seq = lax.axis_index("seq")
    row_ids = jnp.arange(rows, dtype=jnp.int32)
    indices = me_seq * rows + row_ids
    segment, frame_pos, row_pos, col_pos = token_layout(indices, frame_counts)
    modulated = modulate(latents, modulation, segment)
    projected = jnp.dot(
        modulated, w_qkv.reshape(model_width, 3 * width_dev), preferred_element_type=jnp.float32
    )
    q_raw = projected[:, :width_dev]
    k_raw = projected[:, width_dev : 2 * width_dev]
    values = projected[:, 2 * width_dev :].astype(jnp.bfloat16)
    partial_sums = jnp.stack([jnp.sum(q_raw * q_raw, axis=1), jnp.sum(k_raw * k_raw, axis=1)])
    squares = lax.psum(partial_sums, "mp")
    channels = width_dev * lax.axis_size("mp")
    q_norm = q_raw * lax.rsqrt(squares[0] / channels + 1e-06)[:, None] * qk_gains[0][None, :]
    k_norm = k_raw * lax.rsqrt(squares[1] / channels + 1e-06)[:, None] * qk_gains[1][None, :]
    cosine, sine = rope_tables(frame_pos, row_pos, col_pos, HD)
    queries = apply_rotary(q_norm.reshape(rows, heads, HD), cosine, sine).astype(jnp.bfloat16)
    keys = apply_rotary(k_norm.reshape(rows, heads, HD), cosine, sine).astype(jnp.bfloat16)
    stacked = jnp.stack([keys.reshape(rows, width_dev), values])
    initial = (
        jnp.full((heads, rows), mask_floor, jnp.float32),
        jnp.zeros((heads, rows), jnp.float32),
        jnp.zeros((rows, heads, HD), jnp.float32),
    )
    piece = lax.all_gather(stacked, "seq", axis=1, tiled=True)
    key_index = jnp.arange(piece.shape[1], dtype=jnp.int32)
    key_seg = token_layout(key_index, frame_counts)[0]
    state = attend_piece(initial, piece, key_seg, queries, segment)
    maxima, totals, accum = state
    result = accum / jnp.transpose(totals)[:, :, None]
    return result.astype(jnp.bfloat16).reshape(rows, width_dev)


SLOTS = 8
CHUNKS = 4


def rotary_constants(positions):
    sixth_part = HD // 6
    frame_dim = HD - 4 * sixth_part
    side_dim = 2 * sixth_part
    frame_freq = 10000.0 ** (-np.arange(0, frame_dim, 2) / frame_dim)
    side_freq = 10000.0 ** (-np.arange(0, side_dim, 2) / side_dim)
    token = np.arange(FRAME_TOK)
    angles = np.zeros((FRAME_TOK, HD // 2))
    angles[:, frame_dim // 2 : frame_dim // 2 + sixth_part] = (token // GRID_W)[:, None] * side_freq
    angles[:, frame_dim // 2 + sixth_part :] = (token % GRID_W)[:, None] * side_freq
    wide = np.repeat(angles, 2, axis=1)
    lane = np.arange(HD)
    even = (lane % 2 == 0)[None, :]
    side = (lane >= frame_dim)[None, :]
    tables = np.stack(
        [
            np.where(side, np.cos(wide), 0.0),
            np.where(side & even, -np.sin(wide), 0.0),
            np.where(side & ~even, np.sin(wide), 0.0),
        ]
    )
    turns = np.arange(positions)[:, None] * np.repeat(frame_freq, 2)
    turns = np.pad(turns, ((0, 0), (0, HD - frame_dim)))
    rows = np.stack(
        [
            np.where(side, 0.0, np.cos(turns)),
            np.where(even, -np.sin(turns), 0.0),
            np.where(even, 0.0, np.sin(turns)),
        ],
        axis=1,
    )
    return tables.astype(np.float32), rows.astype(np.float32)


def fused_kernel(
    counts_ref, x_hbm, w_hbm, mod_ref, gain_ref, side_ref, table_ref, out_ref,
    bias_ref, frame_ref, xbuf, ybuf, wbuf, kvg, qbuf, acc, rows_mod, squares, rkeys, maxima, totals, accum,
    xsem, wsem, fsem, ssem, rsem, qs_sem, qr_sem, ks_sem, kr_sem,
):
    rows, width = xbuf.shape
    heads = qbuf.shape[1] // HD
    chunk = width // CHUNKS
    me = lax.axis_index("seq")
    me_mp = lax.axis_index("mp")
    n_mp = squares.shape[1]
    channels = heads * HD * n_mp
    frames = rows // FRAME_TOK

    def peer(rel):
        target = me
        for bit in (1, 2, 4):
            if rel & bit:
                target = target + bit - 2 * bit * (me // bit % 2)
        return {"seq": target}

    def peer_mp(rel):
        return {"mp": (me_mp + rel) % n_mp}

    def x_copy(f):
        span = pl.ds(f * FRAME_TOK, FRAME_TOK)
        return pltpu.make_async_copy(x_hbm.at[span], xbuf.at[span], xsem.at[f])

    def w_copy(which, j):
        span = pl.ds(pl.multiple_of(j * chunk, chunk), chunk)
        return pltpu.make_async_copy(
            w_hbm.at[which, span], wbuf.at[which, span], wsem.at[which, j]
        )

    x_copy(0).start()
    for j in range(CHUNKS):
        w_copy(1, j).start()

    barrier = pltpu.get_barrier_semaphore()
    for rel in range(1, SLOTS):
        pl.semaphore_signal(barrier, inc=1, device_id=peer(rel), device_id_type=pl.DeviceIdType.MESH)
    for rel in range(1, n_mp):
        pl.semaphore_signal(barrier, inc=1, device_id=peer_mp(rel), device_id_type=pl.DeviceIdType.MESH)

    ends, starts = [], []
    for s in range(NSEG):
        starts.append(ends[-1] if s else jnp.int32(0))
        ends.append(starts[-1] + counts_ref[s])

    def segment_of(frame):
        return sum(jnp.where(frame >= end, 1, 0) for end in ends)

    own_seg = [segment_of(me * frames + f) for f in range(frames)]
    for rel in range(SLOTS):
        for g in range(frames):
            key_seg = segment_of(peer(rel)["seq"] * frames + g)
            for f in range(frames):
                bias_ref[f, rel * frames + g] = jnp.where(own_seg[f] == key_seg, 0.0, mask_floor)

    for f in range(frames):
        chosen_start = sum(jnp.where(own_seg[f] == s, starts[s], 0) for s in range(NSEG))
        frame_ref[f] = table_ref[jnp.clip(me * frames + f - chosen_start, 0, table_ref.shape[0] - 1)]
        pair = mod_ref[jnp.minimum(own_seg[f], NSEG - 1)]
        rows_mod[2 * f] = jnp.broadcast_to(pair[0:1, :], (8, width))
        rows_mod[2 * f + 1] = jnp.broadcast_to(1.0 + pair[1:2, :], (8, width))

    def norm_frame(f):
        x_copy(f).wait()

        block, lanes = 128, 128
        groups = width // lanes
        for i in range(FRAME_TOK // block):
            span = slice(f * FRAME_TOK + i * block, f * FRAME_TOK + (i + 1) * block)

            def load(k):
                return xbuf[span, k * lanes : (k + 1) * lanes].astype(jnp.float32)

            total = load(0)
            for k in range(1, groups):
                total = total + load(k)
            average = jnp.sum(total, axis=1, keepdims=True) * (1.0 / width)
            power = jnp.zeros((block, lanes), jnp.float32)
            for k in range(groups):
                centred = load(k) - average
                power = power + centred * centred
            variance = jnp.sum(power, axis=1, keepdims=True) * (1.0 / width)
            inverse = lax.rsqrt(variance + 1e-06)
            for k in range(groups):
                cols = slice(k * lanes, (k + 1) * lanes)
                normed = ((load(k) - average) * inverse).reshape(block // 8, 8, lanes)
                scaled = normed * rows_mod[2 * f + 1, :, cols] + rows_mod[2 * f, :, cols]
                ybuf[span, cols] = scaled.reshape(block, lanes).astype(jnp.bfloat16)

    def project(which, first, last, wait):
        if wait:
            for j in range(CHUNKS):
                w_copy(which, j).wait()
        acc[first:last, :] = jnp.dot(ybuf[first:last, :], wbuf[which], preferred_element_type=jnp.float32)

    def row_squares(kind):
        total = jnp.zeros((rows, HD), jnp.float32)
        for h in range(heads):
            piece = acc[:, h * HD : (h + 1) * HD]
            total = total + piece * piece
        squares[kind, 0] = lax.dot_general(
            jnp.ones((8, HD), jnp.float32), total, (((1,), (1,)), ((), ())),
            precision=lax.Precision.HIGHEST, preferred_element_type=jnp.float32,
        )

    def rotate(kind, f, h):
        span = slice(f * FRAME_TOK, (f + 1) * FRAME_TOK)
        lanes = slice(h * HD, (h + 1) * HD)
        value = acc[span, lanes] * gain_ref[kind : kind + 1, lanes]
        cosine = side_ref[0] + frame_ref[f, 0:1, :]
        below = side_ref[1] + frame_ref[f, 1:2, :]
        above = side_ref[2] + frame_ref[f, 2:3, :]
        return value * cosine + pltpu.roll(value, HD - 1, 1) * below + pltpu.roll(value, 1, 1) * above

    key_sends = [(f, rel) for f in range(frames) for rel in (2, 4, 1)]
    first_sends = [(0, 1, 4, 4), (0, 1, 2, 2), (0, 1, 1, 1)]
    later_sends = [
        (2, 0, 4, 6), (4, 1, 2, 6),
        (2, 0, 1, 3), (2, 1, 1, 3), (4, 0, 1, 5), (4, 1, 1, 5),
        (6, 0, 1, 7), (6, 1, 1, 7),
    ]
    sends = first_sends + later_sends

    def send(entry):
        source, part, rel, landing = entry
        return pltpu.make_async_remote_copy(
            src_ref=kvg.at[source, part], dst_ref=kvg.at[landing, part],
            send_sem=ssem.at[sends.index(entry)], recv_sem=rsem.at[landing, part],
            device_id=peer(rel), device_id_type=pl.DeviceIdType.MESH,
        )

    def send_keys(f, rel):
        span = pl.ds(f * FRAME_TOK, FRAME_TOK)
        return pltpu.make_async_remote_copy(
            src_ref=kvg.at[0, 0, span], dst_ref=kvg.at[rel, 0, span],
            send_sem=fsem.at[key_sends.index((f, rel))], recv_sem=rsem.at[rel, 0],
            device_id=peer(rel), device_id_type=pl.DeviceIdType.MESH,
        )

    def arrived(slot, part):
        pltpu.make_async_copy(kvg.at[slot, part], kvg.at[slot, part], rsem.at[slot, part]).wait()

    def send_squares(kind, rel):
        return pltpu.make_async_remote_copy(
            src_ref=squares.at[kind, 0], dst_ref=squares.at[kind, rel],
            send_sem=qs_sem.at[kind, rel], recv_sem=qr_sem.at[kind, rel],
            device_id=peer_mp(rel), device_id_type=pl.DeviceIdType.MESH,
        )

    def send_rkeys(rel):
        return pltpu.make_async_remote_copy(
            src_ref=rkeys.at[0], dst_ref=rkeys.at[rel],
            send_sem=ks_sem.at[rel], recv_sem=kr_sem.at[rel],
            device_id=peer(rel), device_id_type=pl.DeviceIdType.MESH,
        )

    def inverse_rms(kind):
        total = squares[kind, 0]
        for rel in range(1, n_mp):
            send_squares(kind, rel).wait_recv()
            total = total + squares[kind, rel]
        return lax.rsqrt(total * (1.0 / channels) + 1e-06)

    for f in range(frames):
        norm_frame(f)
        if f == 0:
            for j in range(CHUNKS):
                w_copy(1, j).wait()
            for later in range(1, frames):
                x_copy(later).start()
            for which in (2, 0):
                for j in range(CHUNKS):
                    w_copy(which, j).start()
        project(1, f * FRAME_TOK, (f + 1) * FRAME_TOK, False)
        for h in range(heads):
            kvg[0, 0, f * FRAME_TOK : (f + 1) * FRAME_TOK, h * HD : (h + 1) * HD] = rotate(1, f, h).astype(jnp.bfloat16)
        if f == 0:
            pl.semaphore_wait(barrier, SLOTS - 1 + n_mp - 1)
        for rel in (2, 4, 1):
            send_keys(f, rel).start()
    row_squares(1)
    for rel in range(1, n_mp):
        send_squares(1, rel).start()

    project(2, 0, rows, True)
    kvg[0, 1] = acc[...].astype(jnp.bfloat16)
    for entry in first_sends:
        send(entry).start()
    rkeys[0] = inverse_rms(1) * (math.log2(math.e) / math.sqrt(HD))
    for rel in range(1, SLOTS):
        send_rkeys(rel).start()

    project(0, 0, rows, True)
    row_squares(0)
    for rel in range(1, n_mp):
        send_squares(0, rel).start()
    for f in range(frames):
        for h in range(heads):
            accum[f * FRAME_TOK : (f + 1) * FRAME_TOK, h * HD : (h + 1) * HD] = rotate(0, f, h)

    arrived(2, 0)
    send(later_sends[0]).start()
    send(later_sends[2]).start()
    arrived(4, 1)
    send(later_sends[1]).start()
    send(later_sends[5]).start()
    arrived(2, 1)
    send(later_sends[3]).start()
    arrived(4, 0)
    send(later_sends[4]).start()

    rquery = inverse_rms(0)
    column = jnp.transpose(jnp.broadcast_to(rquery[0:1, :], (HD, rows)))
    for h in range(heads):
        lanes = slice(h * HD, (h + 1) * HD)
        qbuf[:, lanes] = (accum[:, lanes] * column).astype(jnp.bfloat16)

    maxima[...] = jnp.full(maxima.shape, mask_floor, jnp.float32)
    totals[...] = jnp.zeros(totals.shape, jnp.float32)
    accum[...] = jnp.zeros(accum.shape, jnp.float32)

    def wait_slot(slot):
        arrived(slot, 0)
        arrived(slot, 1)

    def attend_slot(slot, carry):
        @pl.when(slot > 0)
        def _():
            pltpu.make_async_copy(rkeys.at[slot], rkeys.at[slot], kr_sem.at[slot]).wait()

        @pl.when(jnp.logical_or(slot == 1, jnp.logical_or(slot == 3, slot == 5)))
        def _():
            wait_slot(slot)

        @pl.when(slot == 7)
        def _():
            wait_slot(slot)

        @pl.when(slot == 6)
        def _():
            arrived(6, 0)
            send(later_sends[6]).start()
            arrived(6, 1)
            send(later_sends[7]).start()

        def attend_frame(f, inner):
            span = pl.ds(pl.multiple_of(f * FRAME_TOK, FRAME_TOK), FRAME_TOK)
            lane = lax.broadcasted_iota(jnp.int32, (1, rows), 1)
            shift = jnp.full((1, rows), bias_ref[f, slot * frames], jnp.float32)
            for g in range(1, frames):
                shift = jnp.where(lane >= g * FRAME_TOK, bias_ref[f, slot * frames + g], shift)
            scale = rkeys[slot, 0:1, :]

            def score(h):
                lanes = slice(h * HD, (h + 1) * HD)
                return lax.dot_general(
                    qbuf[span, lanes], kvg[slot, 0, :, lanes], (((1,), (1,)), ((), ())),
                    preferred_element_type=jnp.float32,
                )

            ones = jnp.ones((rows, HD), jnp.bfloat16)
            ahead = score(0)
            for h in range(heads):
                lanes = slice(h * HD, (h + 1) * HD)
                scores = ahead * scale + shift
                if h + 1 < heads:
                    ahead = score(h + 1)
                before = maxima[h, span, :]
                newest = jnp.maximum(before, jnp.max(scores, axis=1, keepdims=True))
                weights = jnp.exp2(scores - newest[:, 0:1]).astype(jnp.bfloat16)
                factor = jnp.exp2(before - newest)
                wide = jnp.concatenate([kvg[slot, 1, :, lanes], ones], axis=1)
                product = jnp.dot(weights, wide, preferred_element_type=jnp.float32)
                totals[h, span, :] = totals[h, span, :] * factor + product[:, HD:]
                accum[span, lanes] = accum[span, lanes] * factor + product[:, :HD]
                maxima[h, span, :] = newest
            return inner

        return lax.fori_loop(0, frames, attend_frame, carry)

    lax.fori_loop(0, SLOTS, attend_slot, 0)
    for h in range(heads):
        lanes = slice(h * HD, (h + 1) * HD)
        out_ref[:, lanes] = (accum[:, lanes] / totals[h]).astype(jnp.bfloat16)

    for f, rel in key_sends:
        send_keys(f, rel).wait_send()
    for entry in sends:
        send(entry).wait_send()
    for rel in range(1, n_mp):
        send_squares(0, rel).wait_send()
        send_squares(1, rel).wait_send()
    for rel in range(1, SLOTS):
        send_rkeys(rel).wait_send()


def fused_body(latents, modulation, w_qkv, qk_gains, frame_counts):
    rows, width = latents.shape
    width_dev = w_qkv.shape[2]
    heads = width_dev // HD
    frames = rows // FRAME_TOK
    n_mp = lax.axis_size("mp")
    side, table = rotary_constants(SLOTS * frames)
    weights = jnp.transpose(w_qkv, (1, 0, 2))
    vmem = pl.BlockSpec(memory_space=pltpu.VMEM)
    smem = pl.BlockSpec(memory_space=pltpu.SMEM)
    hbm = pl.BlockSpec(memory_space=pl.ANY)
    dma = pltpu.SemaphoreType.DMA
    flops = 2 * rows * width * 3 * width_dev + 4 * rows * rows * SLOTS * width_dev
    return pl.pallas_call(
        fused_kernel,
        out_shape=jax.ShapeDtypeStruct((rows, width_dev), jnp.bfloat16),
        in_specs=[smem, hbm, hbm, vmem, vmem, vmem, vmem],
        out_specs=vmem,
        scratch_shapes=[
            pltpu.SMEM((frames, SLOTS * frames), jnp.float32),
            pltpu.VMEM((frames, 3, HD), jnp.float32),
            pltpu.VMEM((rows, width), jnp.bfloat16),
            pltpu.VMEM((rows, width), jnp.bfloat16),
            pltpu.VMEM((3, width, width_dev), jnp.bfloat16),
            pltpu.VMEM((SLOTS, 2, rows, width_dev), jnp.bfloat16),
            pltpu.VMEM((rows, width_dev), jnp.bfloat16),
            pltpu.VMEM((rows, width_dev), jnp.float32),
            pltpu.VMEM((2 * frames, 8, width), jnp.float32),
            pltpu.VMEM((2, n_mp, 8, rows), jnp.float32),
            pltpu.VMEM((SLOTS, 8, rows), jnp.float32),
            pltpu.VMEM((heads, rows, HD), jnp.float32),
            pltpu.VMEM((heads, rows, HD), jnp.float32),
            pltpu.VMEM((rows, width_dev), jnp.float32),
            dma((frames,)),
            dma((3, CHUNKS)),
            dma((3 * frames,)),
            dma((11,)),
            dma((SLOTS, 2)),
            dma((2, n_mp)),
            dma((2, n_mp)),
            dma((SLOTS,)),
            dma((SLOTS,)),
        ],
        compiler_params=pltpu.CompilerParams(
            collective_id=0, has_side_effects=True, vmem_limit_bytes=60 * 1024 * 1024
        ),
        cost_estimate=pl.CostEstimate(flops=flops, bytes_accessed=30000000, transcendentals=12000000),
    )(frame_counts, latents, weights, modulation, qk_gains, side, table)


def solution(mesh):
    in_specs = (P("seq", None), P(), P(None, None, "mp"), P(None, "mp"), P())
    out_specs = P("seq", "mp")
    chosen = fused_body if mesh.shape["seq"] == SLOTS else body
    return jax.shard_map(chosen, mesh=mesh, in_specs=in_specs, out_specs=out_specs, check_vma=False)
```

```python
import math

import jax
import jax.numpy as jnp
import numpy as np
from jax import lax
from jax.experimental import pallas as pl
from jax.experimental.pallas import tpu as pltpu
from jax.sharding import PartitionSpec as P

HD = 128
GRID_W = 16
NSEG = 6
FRAME_TOK = 256


mask_floor = -1e30


def token_layout(indices, frame_counts):
    frames = indices // FRAME_TOK
    lower = np.tril(np.ones((NSEG, NSEG), np.int32))
    ends = jnp.sum(frame_counts[None, :] * lower, axis=1)
    segment = jnp.sum((frames[:, None] >= ends[None, :]).astype(jnp.int32), axis=1)
    starts = ends - frame_counts
    chosen = segment[:, None] == jnp.arange(NSEG, dtype=jnp.int32)[None, :]
    first_frame = jnp.sum(jnp.where(chosen, starts[None, :], 0), axis=1)
    return (segment, frames - first_frame, indices % FRAME_TOK // GRID_W, indices % GRID_W)


def rope_tables(frame_pos, row_pos, col_pos, head_dim):
    sixth_part = head_dim // 6
    frame_dim = head_dim - 4 * sixth_part
    side_dim = 2 * sixth_part
    frame_freq = 10000.0 ** (-np.arange(0, frame_dim, 2) / frame_dim)
    side_freq = 10000.0 ** (-np.arange(0, side_dim, 2) / side_dim)
    empty_frame = np.zeros(frame_dim // 2)
    empty_side = np.zeros(sixth_part)
    along_frame = jnp.asarray(np.concatenate([frame_freq, empty_side, empty_side]), jnp.float32)
    along_rows = jnp.asarray(np.concatenate([empty_frame, side_freq, empty_side]), jnp.float32)
    along_cols = jnp.asarray(np.concatenate([empty_frame, empty_side, side_freq]), jnp.float32)
    angles = (
        frame_pos.astype(jnp.float32)[:, None] * along_frame[None, :]
        + row_pos.astype(jnp.float32)[:, None] * along_rows[None, :]
        + col_pos.astype(jnp.float32)[:, None] * along_cols[None, :]
    )
    return (jnp.cos(angles), jnp.sin(angles))


def apply_rotary(values, cosine, sine):
    shaped = values.reshape(values.shape[0], values.shape[1], -1, 2)
    first_part = shaped[..., 0]
    second_part = shaped[..., 1]
    cos_wide = cosine[:, None, :]
    sin_wide = sine[:, None, :]
    turned = jnp.stack(
        [
            first_part * cos_wide - second_part * sin_wide,
            first_part * sin_wide + second_part * cos_wide,
        ],
        axis=-1,
    )
    return turned.reshape(values.shape)


def modulate(latents, modulation, segment):
    floats = latents.astype(jnp.float32)
    average = jnp.mean(floats, axis=1, keepdims=True)
    centred = floats - average
    variance = jnp.mean(centred * centred, axis=1, keepdims=True)
    normed = centred * lax.rsqrt(variance + 1e-06)
    chosen = (segment[:, None] == jnp.arange(NSEG, dtype=jnp.int32)[None, :]).astype(jnp.float32)
    shifts = jnp.dot(chosen, modulation[:, 0, :], precision=lax.Precision.HIGHEST)
    scales = jnp.dot(chosen, modulation[:, 1, :], precision=lax.Precision.HIGHEST)
    return (normed * (1.0 + scales) + shifts).astype(jnp.bfloat16)


def attend_block(state, key_block, key_segs, queries, query_seg):
    maxima, totals, accum = state
    heads = queries.shape[1]
    keys_three = key_block[0].reshape(-1, heads, HD)
    values_three = key_block[1].reshape(-1, heads, HD)
    scores = jnp.einsum("qhd,khd->hqk", queries, keys_three, preferred_element_type=jnp.float32) * (
        1.0 / math.sqrt(HD)
    )
    allowed = query_seg[None, :, None] == key_segs[None, None, :]
    newest = jnp.maximum(maxima, jnp.max(jnp.where(allowed, scores, mask_floor), axis=2))
    weights = jnp.where(allowed, jnp.exp(scores - newest[:, :, None]), 0.0)
    factor = jnp.exp(maxima - newest)
    totals = totals * factor + jnp.sum(weights, axis=2)
    product = jnp.einsum(
        "hqk,khd->qhd",
        weights.astype(jnp.bfloat16),
        values_three,
        preferred_element_type=jnp.float32,
    )
    accum = accum * jnp.transpose(factor)[:, :, None] + product
    return (newest, totals, accum)


def attend_piece(state, pieces, key_seg, queries, query_seg):
    count_rows = pieces.shape[1]
    span_rows = math.gcd(count_rows, 512)

    def guarded(carried, key_block, key_segs):
        touches = jnp.logical_and(
            jnp.max(key_segs) >= query_seg[0],
            jnp.min(jnp.where(key_segs >= 0, key_segs, NSEG)) <= query_seg[-1],
        )
        return lax.cond(
            touches,
            lambda inner: attend_block(inner, key_block, key_segs, queries, query_seg),
            lambda inner: inner,
            carried,
        )

    def advance(position, carried):
        key_block = lax.dynamic_slice_in_dim(pieces, position * span_rows, span_rows, 1)
        key_segs = lax.dynamic_slice_in_dim(key_seg, position * span_rows, span_rows, 0)
        return guarded(carried, key_block, key_segs)

    return lax.fori_loop(0, count_rows // span_rows, advance, state)


def body(latents, modulation, w_qkv, qk_gains, frame_counts):
    rows = latents.shape[0]
    model_width = latents.shape[1]
    width_dev = w_qkv.shape[2]
    heads = width_dev // HD
    me_seq = lax.axis_index("seq")
    row_ids = jnp.arange(rows, dtype=jnp.int32)
    indices = me_seq * rows + row_ids
    segment, frame_pos, row_pos, col_pos = token_layout(indices, frame_counts)
    modulated = modulate(latents, modulation, segment)
    projected = jnp.dot(
        modulated, w_qkv.reshape(model_width, 3 * width_dev), preferred_element_type=jnp.float32
    )
    q_raw = projected[:, :width_dev]
    k_raw = projected[:, width_dev : 2 * width_dev]
    values = projected[:, 2 * width_dev :].astype(jnp.bfloat16)
    partial_sums = jnp.stack([jnp.sum(q_raw * q_raw, axis=1), jnp.sum(k_raw * k_raw, axis=1)])
    squares = lax.psum(partial_sums, "mp")
    channels = width_dev * lax.axis_size("mp")
    q_norm = q_raw * lax.rsqrt(squares[0] / channels + 1e-06)[:, None] * qk_gains[0][None, :]
    k_norm = k_raw * lax.rsqrt(squares[1] / channels + 1e-06)[:, None] * qk_gains[1][None, :]
    cosine, sine = rope_tables(frame_pos, row_pos, col_pos, HD)
    queries = apply_rotary(q_norm.reshape(rows, heads, HD), cosine, sine).astype(jnp.bfloat16)
    keys = apply_rotary(k_norm.reshape(rows, heads, HD), cosine, sine).astype(jnp.bfloat16)
    stacked = jnp.stack([keys.reshape(rows, width_dev), values])
    initial = (
        jnp.full((heads, rows), mask_floor, jnp.float32),
        jnp.zeros((heads, rows), jnp.float32),
        jnp.zeros((rows, heads, HD), jnp.float32),
    )
    piece = lax.all_gather(stacked, "seq", axis=1, tiled=True)
    key_index = jnp.arange(piece.shape[1], dtype=jnp.int32)
    key_seg = token_layout(key_index, frame_counts)[0]
    state = attend_piece(initial, piece, key_seg, queries, segment)
    maxima, totals, accum = state
    result = accum / jnp.transpose(totals)[:, :, None]
    return result.astype(jnp.bfloat16).reshape(rows, width_dev)


SLOTS = 8
CHUNKS = 4


def rotary_constants(positions):
    sixth_part = HD // 6
    frame_dim = HD - 4 * sixth_part
    side_dim = 2 * sixth_part
    frame_freq = 10000.0 ** (-np.arange(0, frame_dim, 2) / frame_dim)
    side_freq = 10000.0 ** (-np.arange(0, side_dim, 2) / side_dim)
    token = np.arange(FRAME_TOK)
    angles = np.zeros((FRAME_TOK, HD // 2))
    angles[:, frame_dim // 2 : frame_dim // 2 + sixth_part] = (token // GRID_W)[:, None] * side_freq
    angles[:, frame_dim // 2 + sixth_part :] = (token % GRID_W)[:, None] * side_freq
    wide = np.repeat(angles, 2, axis=1)
    lane = np.arange(HD)
    even = (lane % 2 == 0)[None, :]
    side = (lane >= frame_dim)[None, :]
    tables = np.stack(
        [
            np.where(side, np.cos(wide), 0.0),
            np.where(side & even, -np.sin(wide), 0.0),
            np.where(side & ~even, np.sin(wide), 0.0),
        ]
    )
    turns = np.arange(positions)[:, None] * np.repeat(frame_freq, 2)
    turns = np.pad(turns, ((0, 0), (0, HD - frame_dim)))
    rows = np.stack(
        [
            np.where(side, 0.0, np.cos(turns)),
            np.where(even, -np.sin(turns), 0.0),
            np.where(even, 0.0, np.sin(turns)),
        ],
        axis=1,
    )
    return tables.astype(np.float32), rows.astype(np.float32)


def fused_kernel(
    counts_ref, x_hbm, w_hbm, mod_ref, gain_ref, side_ref, table_ref, out_ref,
    bias_ref, frame_ref, xbuf, ybuf, wbuf, kvg, qbuf, acc, rows_mod, squares, rkeys, maxima, totals, accum,
    xsem, wsem, fsem, ssem, rsem, qs_sem, qr_sem, ks_sem, kr_sem,
):
    rows, width = xbuf.shape
    heads = qbuf.shape[1] // HD
    chunk = width // CHUNKS
    me = lax.axis_index("seq")
    me_mp = lax.axis_index("mp")
    n_mp = squares.shape[1]
    channels = heads * HD * n_mp
    frames = rows // FRAME_TOK

    def peer(rel):
        target = me
        for bit in (1, 2, 4):
            if rel & bit:
                target = target + bit - 2 * bit * (me // bit % 2)
        return {"seq": target}

    def peer_mp(rel):
        return {"mp": (me_mp + rel) % n_mp}

    def x_copy(f):
        span = pl.ds(f * FRAME_TOK, FRAME_TOK)
        return pltpu.make_async_copy(x_hbm.at[span], xbuf.at[span], xsem.at[f])

    def w_copy(which, j):
        span = pl.ds(pl.multiple_of(j * chunk, chunk), chunk)
        return pltpu.make_async_copy(
            w_hbm.at[which, span], wbuf.at[which, span], wsem.at[which, j]
        )

    x_copy(0).start()
    for j in range(CHUNKS):
        w_copy(1, j).start()

    barrier = pltpu.get_barrier_semaphore()
    for rel in range(1, SLOTS):
        pl.semaphore_signal(barrier, inc=1, device_id=peer(rel), device_id_type=pl.DeviceIdType.MESH)
    for rel in range(1, n_mp):
        pl.semaphore_signal(barrier, inc=1, device_id=peer_mp(rel), device_id_type=pl.DeviceIdType.MESH)

    ends, starts = [], []
    for s in range(NSEG):
        starts.append(ends[-1] if s else jnp.int32(0))
        ends.append(starts[-1] + counts_ref[s])

    def segment_of(frame):
        return sum(jnp.where(frame >= end, 1, 0) for end in ends)

    own_seg = [segment_of(me * frames + f) for f in range(frames)]
    for rel in range(SLOTS):
        for g in range(frames):
            key_seg = segment_of(peer(rel)["seq"] * frames + g)
            for f in range(frames):
                bias_ref[f, rel * frames + g] = jnp.where(own_seg[f] == key_seg, 0.0, mask_floor)

    for f in range(frames):
        chosen_start = sum(jnp.where(own_seg[f] == s, starts[s], 0) for s in range(NSEG))
        frame_ref[f] = table_ref[jnp.clip(me * frames + f - chosen_start, 0, table_ref.shape[0] - 1)]
        pair = mod_ref[jnp.minimum(own_seg[f], NSEG - 1)]
        rows_mod[2 * f] = jnp.broadcast_to(pair[0:1, :], (8, width))
        rows_mod[2 * f + 1] = jnp.broadcast_to(1.0 + pair[1:2, :], (8, width))

    def norm_frame(f):
        x_copy(f).wait()

        block, lanes = 128, 128
        groups = width // lanes
        for i in range(FRAME_TOK // block):
            span = slice(f * FRAME_TOK + i * block, f * FRAME_TOK + (i + 1) * block)

            def load(k):
                return xbuf[span, k * lanes : (k + 1) * lanes].astype(jnp.float32)

            total = load(0)
            for k in range(1, groups):
                total = total + load(k)
            average = jnp.sum(total, axis=1, keepdims=True) * (1.0 / width)
            power = jnp.zeros((block, lanes), jnp.float32)
            for k in range(groups):
                centred = load(k) - average
                power = power + centred * centred
            variance = jnp.sum(power, axis=1, keepdims=True) * (1.0 / width)
            inverse = lax.rsqrt(variance + 1e-06)
            for k in range(groups):
                cols = slice(k * lanes, (k + 1) * lanes)
                normed = ((load(k) - average) * inverse).reshape(block // 8, 8, lanes)
                scaled = normed * rows_mod[2 * f + 1, :, cols] + rows_mod[2 * f, :, cols]
                ybuf[span, cols] = scaled.reshape(block, lanes).astype(jnp.bfloat16)

    def project(which, first, last, wait):
        if wait:
            for j in range(CHUNKS):
                w_copy(which, j).wait()
        acc[first:last, :] = jnp.dot(ybuf[first:last, :], wbuf[which], preferred_element_type=jnp.float32)

    def row_squares(kind):
        total = jnp.zeros((rows, HD), jnp.float32)
        for h in range(heads):
            piece = acc[:, h * HD : (h + 1) * HD]
            total = total + piece * piece
        squares[kind, 0] = lax.dot_general(
            jnp.ones((8, HD), jnp.float32), total, (((1,), (1,)), ((), ())),
            precision=lax.Precision.HIGHEST, preferred_element_type=jnp.float32,
        )

    def rotate(kind, f, h):
        span = slice(f * FRAME_TOK, (f + 1) * FRAME_TOK)
        lanes = slice(h * HD, (h + 1) * HD)
        value = acc[span, lanes] * gain_ref[kind : kind + 1, lanes]
        cosine = side_ref[0] + frame_ref[f, 0:1, :]
        below = side_ref[1] + frame_ref[f, 1:2, :]
        above = side_ref[2] + frame_ref[f, 2:3, :]
        return value * cosine + pltpu.roll(value, HD - 1, 1) * below + pltpu.roll(value, 1, 1) * above

    key_sends = [(f, rel) for f in range(frames) for rel in (2, 4, 1)]
    first_sends = [(0, 1, 4, 4), (0, 1, 2, 2), (0, 1, 1, 1)]
    later_sends = [
        (2, 0, 4, 6), (4, 1, 2, 6),
        (2, 0, 1, 3), (2, 1, 1, 3), (4, 0, 1, 5), (4, 1, 1, 5),
        (6, 0, 1, 7), (6, 1, 1, 7),
    ]
    sends = first_sends + later_sends

    def send(entry):
        source, part, rel, landing = entry
        return pltpu.make_async_remote_copy(
            src_ref=kvg.at[source, part], dst_ref=kvg.at[landing, part],
            send_sem=ssem.at[sends.index(entry)], recv_sem=rsem.at[landing, part],
            device_id=peer(rel), device_id_type=pl.DeviceIdType.MESH,
        )

    def send_keys(f, rel):
        span = pl.ds(f * FRAME_TOK, FRAME_TOK)
        return pltpu.make_async_remote_copy(
            src_ref=kvg.at[0, 0, span], dst_ref=kvg.at[rel, 0, span],
            send_sem=fsem.at[key_sends.index((f, rel))], recv_sem=rsem.at[rel, 0],
            device_id=peer(rel), device_id_type=pl.DeviceIdType.MESH,
        )

    def arrived(slot, part):
        pltpu.make_async_copy(kvg.at[slot, part], kvg.at[slot, part], rsem.at[slot, part]).wait()

    def send_squares(kind, rel):
        return pltpu.make_async_remote_copy(
            src_ref=squares.at[kind, 0], dst_ref=squares.at[kind, rel],
            send_sem=qs_sem.at[kind, rel], recv_sem=qr_sem.at[kind, rel],
            device_id=peer_mp(rel), device_id_type=pl.DeviceIdType.MESH,
        )

    def send_rkeys(rel):
        return pltpu.make_async_remote_copy(
            src_ref=rkeys.at[0], dst_ref=rkeys.at[rel],
            send_sem=ks_sem.at[rel], recv_sem=kr_sem.at[rel],
            device_id=peer(rel), device_id_type=pl.DeviceIdType.MESH,
        )

    def inverse_rms(kind):
        total = squares[kind, 0]
        for rel in range(1, n_mp):
            send_squares(kind, rel).wait_recv()
            total = total + squares[kind, rel]
        return lax.rsqrt(total * (1.0 / channels) + 1e-06)

    for f in range(frames):
        norm_frame(f)
        if f == 0:
            for j in range(CHUNKS):
                w_copy(1, j).wait()
            for later in range(1, frames):
                x_copy(later).start()
            for which in (2, 0):
                for j in range(CHUNKS):
                    w_copy(which, j).start()
        project(1, f * FRAME_TOK, (f + 1) * FRAME_TOK, False)
        for h in range(heads):
            kvg[0, 0, f * FRAME_TOK : (f + 1) * FRAME_TOK, h * HD : (h + 1) * HD] = rotate(1, f, h).astype(jnp.bfloat16)
        if f == 0:
            pl.semaphore_wait(barrier, SLOTS - 1 + n_mp - 1)
        for rel in (2, 4, 1):
            send_keys(f, rel).start()
    row_squares(1)
    for rel in range(1, n_mp):
        send_squares(1, rel).start()

    project(2, 0, rows, True)
    kvg[0, 1] = acc[...].astype(jnp.bfloat16)
    for entry in first_sends:
        send(entry).start()
    rkeys[0] = inverse_rms(1) * (math.log2(math.e) / math.sqrt(HD))
    for rel in range(1, SLOTS):
        send_rkeys(rel).start()

    project(0, 0, rows, True)
    row_squares(0)
    for rel in range(1, n_mp):
        send_squares(0, rel).start()
    for f in range(frames):
        for h in range(heads):
            accum[f * FRAME_TOK : (f + 1) * FRAME_TOK, h * HD : (h + 1) * HD] = rotate(0, f, h)

    arrived(2, 0)
    send(later_sends[0]).start()
    send(later_sends[2]).start()
    arrived(4, 0)
    send(later_sends[4]).start()

    rquery = inverse_rms(0)
    column = jnp.transpose(jnp.broadcast_to(rquery[0:1, :], (HD, rows)))
    for h in range(heads):
        lanes = slice(h * HD, (h + 1) * HD)
        qbuf[:, lanes] = (accum[:, lanes] * column).astype(jnp.bfloat16)

    maxima[...] = jnp.full(maxima.shape, mask_floor, jnp.float32)
    totals[...] = jnp.zeros(totals.shape, jnp.float32)
    accum[...] = jnp.zeros(accum.shape, jnp.float32)

    def wait_slot(slot):
        arrived(slot, 0)
        arrived(slot, 1)

    def attend_slot(slot, carry):
        @pl.when(slot > 0)
        def _():
            pltpu.make_async_copy(rkeys.at[slot], rkeys.at[slot], kr_sem.at[slot]).wait()

        @pl.when(slot == 2)
        def _():
            arrived(4, 1)
            send(later_sends[1]).start()
            send(later_sends[5]).start()
            arrived(2, 1)
            send(later_sends[3]).start()

        @pl.when(jnp.logical_or(slot == 1, jnp.logical_or(slot == 3, slot == 5)))
        def _():
            wait_slot(slot)

        @pl.when(slot == 7)
        def _():
            wait_slot(slot)

        @pl.when(slot == 6)
        def _():
            arrived(6, 0)
            send(later_sends[6]).start()
            arrived(6, 1)
            send(later_sends[7]).start()

        def attend_frame(f, inner):
            span = pl.ds(pl.multiple_of(f * FRAME_TOK, FRAME_TOK), FRAME_TOK)
            lane = lax.broadcasted_iota(jnp.int32, (1, rows), 1)
            shift = jnp.full((1, rows), bias_ref[f, slot * frames], jnp.float32)
            for g in range(1, frames):
                shift = jnp.where(lane >= g * FRAME_TOK, bias_ref[f, slot * frames + g], shift)
            scale = rkeys[slot, 0:1, :]

            def score(h):
                lanes = slice(h * HD, (h + 1) * HD)
                return lax.dot_general(
                    qbuf[span, lanes], kvg[slot, 0, :, lanes], (((1,), (1,)), ((), ())),
                    preferred_element_type=jnp.float32,
                )

            ones = jnp.ones((rows, HD), jnp.bfloat16)
            ahead = score(0)
            for h in range(heads):
                lanes = slice(h * HD, (h + 1) * HD)
                scores = ahead * scale + shift
                if h + 1 < heads:
                    ahead = score(h + 1)
                before = maxima[h, span, :]
                newest = jnp.maximum(before, jnp.max(scores, axis=1, keepdims=True))
                weights = jnp.exp2(scores - newest[:, 0:1]).astype(jnp.bfloat16)
                factor = jnp.exp2(before - newest)
                wide = jnp.concatenate([kvg[slot, 1, :, lanes], ones], axis=1)
                product = jnp.dot(weights, wide, preferred_element_type=jnp.float32)
                totals[h, span, :] = totals[h, span, :] * factor + product[:, HD:]
                accum[span, lanes] = accum[span, lanes] * factor + product[:, :HD]
                maxima[h, span, :] = newest
            return inner

        return lax.fori_loop(0, frames, attend_frame, carry)

    lax.fori_loop(0, SLOTS, attend_slot, 0)
    for h in range(heads):
        lanes = slice(h * HD, (h + 1) * HD)
        out_ref[:, lanes] = (accum[:, lanes] / totals[h]).astype(jnp.bfloat16)

    for f, rel in key_sends:
        send_keys(f, rel).wait_send()
    for entry in sends:
        send(entry).wait_send()
    for rel in range(1, n_mp):
        send_squares(0, rel).wait_send()
        send_squares(1, rel).wait_send()
    for rel in range(1, SLOTS):
        send_rkeys(rel).wait_send()


def fused_body(latents, modulation, w_qkv, qk_gains, frame_counts):
    rows, width = latents.shape
    width_dev = w_qkv.shape[2]
    heads = width_dev // HD
    frames = rows // FRAME_TOK
    n_mp = lax.axis_size("mp")
    side, table = rotary_constants(SLOTS * frames)
    weights = jnp.transpose(w_qkv, (1, 0, 2))
    vmem = pl.BlockSpec(memory_space=pltpu.VMEM)
    smem = pl.BlockSpec(memory_space=pltpu.SMEM)
    hbm = pl.BlockSpec(memory_space=pl.ANY)
    dma = pltpu.SemaphoreType.DMA
    flops = 2 * rows * width * 3 * width_dev + 4 * rows * rows * SLOTS * width_dev
    return pl.pallas_call(
        fused_kernel,
        out_shape=jax.ShapeDtypeStruct((rows, width_dev), jnp.bfloat16),
        in_specs=[smem, hbm, hbm, vmem, vmem, vmem, vmem],
        out_specs=vmem,
        scratch_shapes=[
            pltpu.SMEM((frames, SLOTS * frames), jnp.float32),
            pltpu.VMEM((frames, 3, HD), jnp.float32),
            pltpu.VMEM((rows, width), jnp.bfloat16),
            pltpu.VMEM((rows, width), jnp.bfloat16),
            pltpu.VMEM((3, width, width_dev), jnp.bfloat16),
            pltpu.VMEM((SLOTS, 2, rows, width_dev), jnp.bfloat16),
            pltpu.VMEM((rows, width_dev), jnp.bfloat16),
            pltpu.VMEM((rows, width_dev), jnp.float32),
            pltpu.VMEM((2 * frames, 8, width), jnp.float32),
            pltpu.VMEM((2, n_mp, 8, rows), jnp.float32),
            pltpu.VMEM((SLOTS, 8, rows), jnp.float32),
            pltpu.VMEM((heads, rows, HD), jnp.float32),
            pltpu.VMEM((heads, rows, HD), jnp.float32),
            pltpu.VMEM((rows, width_dev), jnp.float32),
            dma((frames,)),
            dma((3, CHUNKS)),
            dma((3 * frames,)),
            dma((11,)),
            dma((SLOTS, 2)),
            dma((2, n_mp)),
            dma((2, n_mp)),
            dma((SLOTS,)),
            dma((SLOTS,)),
        ],
        compiler_params=pltpu.CompilerParams(
            collective_id=0, has_side_effects=True, vmem_limit_bytes=60 * 1024 * 1024
        ),
        cost_estimate=pl.CostEstimate(flops=flops, bytes_accessed=30000000, transcendentals=12000000),
    )(frame_counts, latents, weights, modulation, qk_gains, side, table)


def solution(mesh):
    in_specs = (P("seq", None), P(), P(None, None, "mp"), P(None, "mp"), P())
    out_specs = P("seq", "mp")
    chosen = fused_body if mesh.shape["seq"] == SLOTS else body
    return jax.shard_map(chosen, mesh=mesh, in_specs=in_specs, out_specs=out_specs, check_vma=False)
```

```python
import math

import jax
import jax.numpy as jnp
import numpy as np
from jax import lax
from jax.experimental import pallas as pl
from jax.experimental.pallas import tpu as pltpu
from jax.sharding import PartitionSpec as P

HD = 128
GRID_W = 16
NSEG = 6
FRAME_TOK = 256


mask_floor = -1e30


def token_layout(indices, frame_counts):
    frames = indices // FRAME_TOK
    lower = np.tril(np.ones((NSEG, NSEG), np.int32))
    ends = jnp.sum(frame_counts[None, :] * lower, axis=1)
    segment = jnp.sum((frames[:, None] >= ends[None, :]).astype(jnp.int32), axis=1)
    starts = ends - frame_counts
    chosen = segment[:, None] == jnp.arange(NSEG, dtype=jnp.int32)[None, :]
    first_frame = jnp.sum(jnp.where(chosen, starts[None, :], 0), axis=1)
    return (segment, frames - first_frame, indices % FRAME_TOK // GRID_W, indices % GRID_W)


def rope_tables(frame_pos, row_pos, col_pos, head_dim):
    sixth_part = head_dim // 6
    frame_dim = head_dim - 4 * sixth_part
    side_dim = 2 * sixth_part
    frame_freq = 10000.0 ** (-np.arange(0, frame_dim, 2) / frame_dim)
    side_freq = 10000.0 ** (-np.arange(0, side_dim, 2) / side_dim)
    empty_frame = np.zeros(frame_dim // 2)
    empty_side = np.zeros(sixth_part)
    along_frame = jnp.asarray(np.concatenate([frame_freq, empty_side, empty_side]), jnp.float32)
    along_rows = jnp.asarray(np.concatenate([empty_frame, side_freq, empty_side]), jnp.float32)
    along_cols = jnp.asarray(np.concatenate([empty_frame, empty_side, side_freq]), jnp.float32)
    angles = (
        frame_pos.astype(jnp.float32)[:, None] * along_frame[None, :]
        + row_pos.astype(jnp.float32)[:, None] * along_rows[None, :]
        + col_pos.astype(jnp.float32)[:, None] * along_cols[None, :]
    )
    return (jnp.cos(angles), jnp.sin(angles))


def apply_rotary(values, cosine, sine):
    shaped = values.reshape(values.shape[0], values.shape[1], -1, 2)
    first_part = shaped[..., 0]
    second_part = shaped[..., 1]
    cos_wide = cosine[:, None, :]
    sin_wide = sine[:, None, :]
    turned = jnp.stack(
        [
            first_part * cos_wide - second_part * sin_wide,
            first_part * sin_wide + second_part * cos_wide,
        ],
        axis=-1,
    )
    return turned.reshape(values.shape)


def modulate(latents, modulation, segment):
    floats = latents.astype(jnp.float32)
    average = jnp.mean(floats, axis=1, keepdims=True)
    centred = floats - average
    variance = jnp.mean(centred * centred, axis=1, keepdims=True)
    normed = centred * lax.rsqrt(variance + 1e-06)
    chosen = (segment[:, None] == jnp.arange(NSEG, dtype=jnp.int32)[None, :]).astype(jnp.float32)
    shifts = jnp.dot(chosen, modulation[:, 0, :], precision=lax.Precision.HIGHEST)
    scales = jnp.dot(chosen, modulation[:, 1, :], precision=lax.Precision.HIGHEST)
    return (normed * (1.0 + scales) + shifts).astype(jnp.bfloat16)


def attend_block(state, key_block, key_segs, queries, query_seg):
    maxima, totals, accum = state
    heads = queries.shape[1]
    keys_three = key_block[0].reshape(-1, heads, HD)
    values_three = key_block[1].reshape(-1, heads, HD)
    scores = jnp.einsum("qhd,khd->hqk", queries, keys_three, preferred_element_type=jnp.float32) * (
        1.0 / math.sqrt(HD)
    )
    allowed = query_seg[None, :, None] == key_segs[None, None, :]
    newest = jnp.maximum(maxima, jnp.max(jnp.where(allowed, scores, mask_floor), axis=2))
    weights = jnp.where(allowed, jnp.exp(scores - newest[:, :, None]), 0.0)
    factor = jnp.exp(maxima - newest)
    totals = totals * factor + jnp.sum(weights, axis=2)
    product = jnp.einsum(
        "hqk,khd->qhd",
        weights.astype(jnp.bfloat16),
        values_three,
        preferred_element_type=jnp.float32,
    )
    accum = accum * jnp.transpose(factor)[:, :, None] + product
    return (newest, totals, accum)


def attend_piece(state, pieces, key_seg, queries, query_seg):
    count_rows = pieces.shape[1]
    span_rows = math.gcd(count_rows, 512)

    def guarded(carried, key_block, key_segs):
        touches = jnp.logical_and(
            jnp.max(key_segs) >= query_seg[0],
            jnp.min(jnp.where(key_segs >= 0, key_segs, NSEG)) <= query_seg[-1],
        )
        return lax.cond(
            touches,
            lambda inner: attend_block(inner, key_block, key_segs, queries, query_seg),
            lambda inner: inner,
            carried,
        )

    def advance(position, carried):
        key_block = lax.dynamic_slice_in_dim(pieces, position * span_rows, span_rows, 1)
        key_segs = lax.dynamic_slice_in_dim(key_seg, position * span_rows, span_rows, 0)
        return guarded(carried, key_block, key_segs)

    return lax.fori_loop(0, count_rows // span_rows, advance, state)


def body(latents, modulation, w_qkv, qk_gains, frame_counts):
    rows = latents.shape[0]
    model_width = latents.shape[1]
    width_dev = w_qkv.shape[2]
    heads = width_dev // HD
    me_seq = lax.axis_index("seq")
    row_ids = jnp.arange(rows, dtype=jnp.int32)
    indices = me_seq * rows + row_ids
    segment, frame_pos, row_pos, col_pos = token_layout(indices, frame_counts)
    modulated = modulate(latents, modulation, segment)
    projected = jnp.dot(
        modulated, w_qkv.reshape(model_width, 3 * width_dev), preferred_element_type=jnp.float32
    )
    q_raw = projected[:, :width_dev]
    k_raw = projected[:, width_dev : 2 * width_dev]
    values = projected[:, 2 * width_dev :].astype(jnp.bfloat16)
    partial_sums = jnp.stack([jnp.sum(q_raw * q_raw, axis=1), jnp.sum(k_raw * k_raw, axis=1)])
    squares = lax.psum(partial_sums, "mp")
    channels = width_dev * lax.axis_size("mp")
    q_norm = q_raw * lax.rsqrt(squares[0] / channels + 1e-06)[:, None] * qk_gains[0][None, :]
    k_norm = k_raw * lax.rsqrt(squares[1] / channels + 1e-06)[:, None] * qk_gains[1][None, :]
    cosine, sine = rope_tables(frame_pos, row_pos, col_pos, HD)
    queries = apply_rotary(q_norm.reshape(rows, heads, HD), cosine, sine).astype(jnp.bfloat16)
    keys = apply_rotary(k_norm.reshape(rows, heads, HD), cosine, sine).astype(jnp.bfloat16)
    stacked = jnp.stack([keys.reshape(rows, width_dev), values])
    initial = (
        jnp.full((heads, rows), mask_floor, jnp.float32),
        jnp.zeros((heads, rows), jnp.float32),
        jnp.zeros((rows, heads, HD), jnp.float32),
    )
    piece = lax.all_gather(stacked, "seq", axis=1, tiled=True)
    key_index = jnp.arange(piece.shape[1], dtype=jnp.int32)
    key_seg = token_layout(key_index, frame_counts)[0]
    state = attend_piece(initial, piece, key_seg, queries, segment)
    maxima, totals, accum = state
    result = accum / jnp.transpose(totals)[:, :, None]
    return result.astype(jnp.bfloat16).reshape(rows, width_dev)


SLOTS = 8
CHUNKS = 4


def rotary_constants(positions):
    sixth_part = HD // 6
    frame_dim = HD - 4 * sixth_part
    side_dim = 2 * sixth_part
    frame_freq = 10000.0 ** (-np.arange(0, frame_dim, 2) / frame_dim)
    side_freq = 10000.0 ** (-np.arange(0, side_dim, 2) / side_dim)
    token = np.arange(FRAME_TOK)
    angles = np.zeros((FRAME_TOK, HD // 2))
    angles[:, frame_dim // 2 : frame_dim // 2 + sixth_part] = (token // GRID_W)[:, None] * side_freq
    angles[:, frame_dim // 2 + sixth_part :] = (token % GRID_W)[:, None] * side_freq
    wide = np.repeat(angles, 2, axis=1)
    lane = np.arange(HD)
    even = (lane % 2 == 0)[None, :]
    side = (lane >= frame_dim)[None, :]
    tables = np.stack(
        [
            np.where(side, np.cos(wide), 0.0),
            np.where(side & even, -np.sin(wide), 0.0),
            np.where(side & ~even, np.sin(wide), 0.0),
        ]
    )
    turns = np.arange(positions)[:, None] * np.repeat(frame_freq, 2)
    turns = np.pad(turns, ((0, 0), (0, HD - frame_dim)))
    rows = np.stack(
        [
            np.where(side, 0.0, np.cos(turns)),
            np.where(even, -np.sin(turns), 0.0),
            np.where(even, 0.0, np.sin(turns)),
        ],
        axis=1,
    )
    return tables.astype(np.float32), rows.astype(np.float32)


def fused_kernel(
    counts_ref, x_hbm, w_hbm, mod_ref, gain_ref, side_ref, table_ref, out_ref,
    bias_ref, frame_ref, xbuf, ybuf, wbuf, kvg, qbuf, acc, rows_mod, squares, rkeys, maxima, totals, accum,
    xsem, wsem, fsem, ssem, rsem, qs_sem, qr_sem, ks_sem, kr_sem,
):
    rows, width = xbuf.shape
    heads = qbuf.shape[1] // HD
    chunk = width // CHUNKS
    me = lax.axis_index("seq")
    me_mp = lax.axis_index("mp")
    n_mp = squares.shape[1]
    channels = heads * HD * n_mp
    frames = rows // FRAME_TOK

    def peer(rel):
        target = me
        for bit in (1, 2, 4):
            if rel & bit:
                target = target + bit - 2 * bit * (me // bit % 2)
        return {"seq": target}

    def peer_mp(rel):
        return {"mp": (me_mp + rel) % n_mp}

    def x_copy(f):
        span = pl.ds(f * FRAME_TOK, FRAME_TOK)
        return pltpu.make_async_copy(x_hbm.at[span], xbuf.at[span], xsem.at[f])

    def w_copy(which, j):
        span = pl.ds(pl.multiple_of(j * chunk, chunk), chunk)
        return pltpu.make_async_copy(
            w_hbm.at[which, span], wbuf.at[which, span], wsem.at[which, j]
        )

    x_copy(0).start()
    for j in range(CHUNKS):
        w_copy(1, j).start()

    barrier = pltpu.get_barrier_semaphore()
    for rel in range(1, SLOTS):
        pl.semaphore_signal(barrier, inc=1, device_id=peer(rel), device_id_type=pl.DeviceIdType.MESH)
    for rel in range(1, n_mp):
        pl.semaphore_signal(barrier, inc=1, device_id=peer_mp(rel), device_id_type=pl.DeviceIdType.MESH)

    ends, starts = [], []
    for s in range(NSEG):
        starts.append(ends[-1] if s else jnp.int32(0))
        ends.append(starts[-1] + counts_ref[s])

    def segment_of(frame):
        return sum(jnp.where(frame >= end, 1, 0) for end in ends)

    own_seg = [segment_of(me * frames + f) for f in range(frames)]
    for rel in range(SLOTS):
        for g in range(frames):
            key_seg = segment_of(peer(rel)["seq"] * frames + g)
            for f in range(frames):
                bias_ref[f, rel * frames + g] = jnp.where(own_seg[f] == key_seg, 0.0, mask_floor)

    for f in range(frames):
        chosen_start = sum(jnp.where(own_seg[f] == s, starts[s], 0) for s in range(NSEG))
        frame_ref[f] = table_ref[jnp.clip(me * frames + f - chosen_start, 0, table_ref.shape[0] - 1)]
        pair = mod_ref[jnp.minimum(own_seg[f], NSEG - 1)]
        rows_mod[2 * f] = jnp.broadcast_to(pair[0:1, :], (8, width))
        rows_mod[2 * f + 1] = jnp.broadcast_to(1.0 + pair[1:2, :], (8, width))

    def norm_frame(f):
        x_copy(f).wait()

        block, lanes = 128, 128
        groups = width // lanes
        for i in range(FRAME_TOK // block):
            span = slice(f * FRAME_TOK + i * block, f * FRAME_TOK + (i + 1) * block)

            def load(k):
                return xbuf[span, k * lanes : (k + 1) * lanes].astype(jnp.float32)

            total = load(0)
            for k in range(1, groups):
                total = total + load(k)
            average = jnp.sum(total, axis=1, keepdims=True) * (1.0 / width)
            power = jnp.zeros((block, lanes), jnp.float32)
            for k in range(groups):
                centred = load(k) - average
                power = power + centred * centred
            variance = jnp.sum(power, axis=1, keepdims=True) * (1.0 / width)
            inverse = lax.rsqrt(variance + 1e-06)
            for k in range(groups):
                cols = slice(k * lanes, (k + 1) * lanes)
                normed = ((load(k) - average) * inverse).reshape(block // 8, 8, lanes)
                scaled = normed * rows_mod[2 * f + 1, :, cols] + rows_mod[2 * f, :, cols]
                ybuf[span, cols] = scaled.reshape(block, lanes).astype(jnp.bfloat16)

    def project(which, first, last, wait):
        if wait:
            for j in range(CHUNKS):
                w_copy(which, j).wait()
        acc[first:last, :] = jnp.dot(ybuf[first:last, :], wbuf[which], preferred_element_type=jnp.float32)

    def row_squares(kind):
        total = jnp.zeros((rows, HD), jnp.float32)
        for h in range(heads):
            piece = acc[:, h * HD : (h + 1) * HD]
            total = total + piece * piece
        squares[kind, 0] = lax.dot_general(
            jnp.ones((8, HD), jnp.float32), total, (((1,), (1,)), ((), ())),
            precision=lax.Precision.HIGHEST, preferred_element_type=jnp.float32,
        )

    def rotate(kind, f, h):
        span = slice(f * FRAME_TOK, (f + 1) * FRAME_TOK)
        lanes = slice(h * HD, (h + 1) * HD)
        value = acc[span, lanes] * gain_ref[kind : kind + 1, lanes]
        cosine = side_ref[0] + frame_ref[f, 0:1, :]
        below = side_ref[1] + frame_ref[f, 1:2, :]
        above = side_ref[2] + frame_ref[f, 2:3, :]
        return value * cosine + pltpu.roll(value, HD - 1, 1) * below + pltpu.roll(value, 1, 1) * above

    key_sends = [(f, rel) for f in range(frames) for rel in (2, 4, 1)]
    first_sends = [(0, 1, 4, 4), (0, 1, 2, 2), (0, 1, 1, 1)]
    later_sends = [
        (2, 0, 4, 6), (4, 1, 2, 6),
        (2, 0, 1, 3), (2, 1, 1, 3), (4, 0, 1, 5), (4, 1, 1, 5),
        (6, 0, 1, 7), (6, 1, 1, 7),
    ]
    sends = first_sends + later_sends

    def send(entry):
        source, part, rel, landing = entry
        return pltpu.make_async_remote_copy(
            src_ref=kvg.at[source, part], dst_ref=kvg.at[landing, part],
            send_sem=ssem.at[sends.index(entry)], recv_sem=rsem.at[landing, part],
            device_id=peer(rel), device_id_type=pl.DeviceIdType.MESH,
        )

    def send_keys(f, rel):
        span = pl.ds(f * FRAME_TOK, FRAME_TOK)
        return pltpu.make_async_remote_copy(
            src_ref=kvg.at[0, 0, span], dst_ref=kvg.at[rel, 0, span],
            send_sem=fsem.at[key_sends.index((f, rel))], recv_sem=rsem.at[rel, 0],
            device_id=peer(rel), device_id_type=pl.DeviceIdType.MESH,
        )

    def arrived(slot, part):
        pltpu.make_async_copy(kvg.at[slot, part], kvg.at[slot, part], rsem.at[slot, part]).wait()

    def send_squares(kind, rel):
        return pltpu.make_async_remote_copy(
            src_ref=squares.at[kind, 0], dst_ref=squares.at[kind, rel],
            send_sem=qs_sem.at[kind, rel], recv_sem=qr_sem.at[kind, rel],
            device_id=peer_mp(rel), device_id_type=pl.DeviceIdType.MESH,
        )

    def send_rkeys(rel):
        return pltpu.make_async_remote_copy(
            src_ref=rkeys.at[0], dst_ref=rkeys.at[rel],
            send_sem=ks_sem.at[rel], recv_sem=kr_sem.at[rel],
            device_id=peer(rel), device_id_type=pl.DeviceIdType.MESH,
        )

    def inverse_rms(kind):
        total = squares[kind, 0]
        for rel in range(1, n_mp):
            send_squares(kind, rel).wait_recv()
            total = total + squares[kind, rel]
        return lax.rsqrt(total * (1.0 / channels) + 1e-06)

    for f in range(frames):
        norm_frame(f)
        if f == 0:
            for j in range(CHUNKS):
                w_copy(1, j).wait()
            for later in range(1, frames):
                x_copy(later).start()
            for which in (2, 0):
                for j in range(CHUNKS):
                    w_copy(which, j).start()
        project(1, f * FRAME_TOK, (f + 1) * FRAME_TOK, False)
        for h in range(heads):
            kvg[0, 0, f * FRAME_TOK : (f + 1) * FRAME_TOK, h * HD : (h + 1) * HD] = rotate(1, f, h).astype(jnp.bfloat16)
        if f == 0:
            pl.semaphore_wait(barrier, SLOTS - 1 + n_mp - 1)
        for rel in (2, 4, 1):
            send_keys(f, rel).start()
    row_squares(1)
    for rel in range(1, n_mp):
        send_squares(1, rel).start()

    project(2, 0, rows, True)
    kvg[0, 1] = acc[...].astype(jnp.bfloat16)
    for entry in first_sends:
        send(entry).start()
    rkeys[0] = inverse_rms(1) * (math.log2(math.e) / math.sqrt(HD))
    for rel in range(1, SLOTS):
        send_rkeys(rel).start()

    project(0, 0, rows, True)
    row_squares(0)
    for rel in range(1, n_mp):
        send_squares(0, rel).start()
    for f in range(frames):
        for h in range(heads):
            accum[f * FRAME_TOK : (f + 1) * FRAME_TOK, h * HD : (h + 1) * HD] = rotate(0, f, h)

    arrived(2, 0)
    send(later_sends[2]).start()
    arrived(4, 0)
    send(later_sends[4]).start()

    rquery = inverse_rms(0)
    column = jnp.transpose(jnp.broadcast_to(rquery[0:1, :], (HD, rows)))
    for h in range(heads):
        lanes = slice(h * HD, (h + 1) * HD)
        qbuf[:, lanes] = (accum[:, lanes] * column).astype(jnp.bfloat16)

    maxima[...] = jnp.full(maxima.shape, mask_floor, jnp.float32)
    totals[...] = jnp.zeros(totals.shape, jnp.float32)
    accum[...] = jnp.zeros(accum.shape, jnp.float32)

    def wait_slot(slot):
        arrived(slot, 0)
        arrived(slot, 1)

    def attend_slot(slot, carry):
        @pl.when(slot > 0)
        def _():
            pltpu.make_async_copy(rkeys.at[slot], rkeys.at[slot], kr_sem.at[slot]).wait()

        @pl.when(slot == 2)
        def _():
            arrived(4, 1)
            send(later_sends[1]).start()
            send(later_sends[0]).start()
            send(later_sends[5]).start()
            arrived(2, 1)
            send(later_sends[3]).start()

        @pl.when(jnp.logical_or(slot == 1, jnp.logical_or(slot == 3, slot == 5)))
        def _():
            wait_slot(slot)

        @pl.when(slot == 7)
        def _():
            wait_slot(slot)

        @pl.when(slot == 6)
        def _():
            arrived(6, 0)
            send(later_sends[6]).start()
            arrived(6, 1)
            send(later_sends[7]).start()

        def attend_frame(f, inner):
            span = pl.ds(pl.multiple_of(f * FRAME_TOK, FRAME_TOK), FRAME_TOK)
            lane = lax.broadcasted_iota(jnp.int32, (1, rows), 1)
            shift = jnp.full((1, rows), bias_ref[f, slot * frames], jnp.float32)
            for g in range(1, frames):
                shift = jnp.where(lane >= g * FRAME_TOK, bias_ref[f, slot * frames + g], shift)
            scale = rkeys[slot, 0:1, :]

            def score(h):
                lanes = slice(h * HD, (h + 1) * HD)
                return lax.dot_general(
                    qbuf[span, lanes], kvg[slot, 0, :, lanes], (((1,), (1,)), ((), ())),
                    preferred_element_type=jnp.float32,
                )

            ones = jnp.ones((rows, HD), jnp.bfloat16)
            ahead = score(0)
            for h in range(heads):
                lanes = slice(h * HD, (h + 1) * HD)
                scores = ahead * scale + shift
                if h + 1 < heads:
                    ahead = score(h + 1)
                before = maxima[h, span, :]
                newest = jnp.maximum(before, jnp.max(scores, axis=1, keepdims=True))
                weights = jnp.exp2(scores - newest[:, 0:1]).astype(jnp.bfloat16)
                factor = jnp.exp2(before - newest)
                wide = jnp.concatenate([kvg[slot, 1, :, lanes], ones], axis=1)
                product = jnp.dot(weights, wide, preferred_element_type=jnp.float32)
                totals[h, span, :] = totals[h, span, :] * factor + product[:, HD:]
                accum[span, lanes] = accum[span, lanes] * factor + product[:, :HD]
                maxima[h, span, :] = newest
            return inner

        return lax.fori_loop(0, frames, attend_frame, carry)

    lax.fori_loop(0, SLOTS, attend_slot, 0)
    for h in range(heads):
        lanes = slice(h * HD, (h + 1) * HD)
        out_ref[:, lanes] = (accum[:, lanes] / totals[h]).astype(jnp.bfloat16)

    for f, rel in key_sends:
        send_keys(f, rel).wait_send()
    for entry in sends:
        send(entry).wait_send()
    for rel in range(1, n_mp):
        send_squares(0, rel).wait_send()
        send_squares(1, rel).wait_send()
    for rel in range(1, SLOTS):
        send_rkeys(rel).wait_send()


def fused_body(latents, modulation, w_qkv, qk_gains, frame_counts):
    rows, width = latents.shape
    width_dev = w_qkv.shape[2]
    heads = width_dev // HD
    frames = rows // FRAME_TOK
    n_mp = lax.axis_size("mp")
    side, table = rotary_constants(SLOTS * frames)
    weights = jnp.transpose(w_qkv, (1, 0, 2))
    vmem = pl.BlockSpec(memory_space=pltpu.VMEM)
    smem = pl.BlockSpec(memory_space=pltpu.SMEM)
    hbm = pl.BlockSpec(memory_space=pl.ANY)
    dma = pltpu.SemaphoreType.DMA
    flops = 2 * rows * width * 3 * width_dev + 4 * rows * rows * SLOTS * width_dev
    return pl.pallas_call(
        fused_kernel,
        out_shape=jax.ShapeDtypeStruct((rows, width_dev), jnp.bfloat16),
        in_specs=[smem, hbm, hbm, vmem, vmem, vmem, vmem],
        out_specs=vmem,
        scratch_shapes=[
            pltpu.SMEM((frames, SLOTS * frames), jnp.float32),
            pltpu.VMEM((frames, 3, HD), jnp.float32),
            pltpu.VMEM((rows, width), jnp.bfloat16),
            pltpu.VMEM((rows, width), jnp.bfloat16),
            pltpu.VMEM((3, width, width_dev), jnp.bfloat16),
            pltpu.VMEM((SLOTS, 2, rows, width_dev), jnp.bfloat16),
            pltpu.VMEM((rows, width_dev), jnp.bfloat16),
            pltpu.VMEM((rows, width_dev), jnp.float32),
            pltpu.VMEM((2 * frames, 8, width), jnp.float32),
            pltpu.VMEM((2, n_mp, 8, rows), jnp.float32),
            pltpu.VMEM((SLOTS, 8, rows), jnp.float32),
            pltpu.VMEM((heads, rows, HD), jnp.float32),
            pltpu.VMEM((heads, rows, HD), jnp.float32),
            pltpu.VMEM((rows, width_dev), jnp.float32),
            dma((frames,)),
            dma((3, CHUNKS)),
            dma((3 * frames,)),
            dma((11,)),
            dma((SLOTS, 2)),
            dma((2, n_mp)),
            dma((2, n_mp)),
            dma((SLOTS,)),
            dma((SLOTS,)),
        ],
        compiler_params=pltpu.CompilerParams(
            collective_id=0, has_side_effects=True, vmem_limit_bytes=60 * 1024 * 1024
        ),
        cost_estimate=pl.CostEstimate(flops=flops, bytes_accessed=30000000, transcendentals=12000000),
    )(frame_counts, latents, weights, modulation, qk_gains, side, table)


def solution(mesh):
    in_specs = (P("seq", None), P(), P(None, None, "mp"), P(None, "mp"), P())
    out_specs = P("seq", "mp")
    chosen = fused_body if mesh.shape["seq"] == SLOTS else body
    return jax.shard_map(chosen, mesh=mesh, in_specs=in_specs, out_specs=out_specs, check_vma=False)
```

```python
import math

import jax
import jax.numpy as jnp
import numpy as np
from jax import lax
from jax.experimental import pallas as pl
from jax.experimental.pallas import tpu as pltpu
from jax.sharding import PartitionSpec as P

HD = 128
GRID_W = 16
NSEG = 6
FRAME_TOK = 256


mask_floor = -1e30


def token_layout(indices, frame_counts):
    frames = indices // FRAME_TOK
    lower = np.tril(np.ones((NSEG, NSEG), np.int32))
    ends = jnp.sum(frame_counts[None, :] * lower, axis=1)
    segment = jnp.sum((frames[:, None] >= ends[None, :]).astype(jnp.int32), axis=1)
    starts = ends - frame_counts
    chosen = segment[:, None] == jnp.arange(NSEG, dtype=jnp.int32)[None, :]
    first_frame = jnp.sum(jnp.where(chosen, starts[None, :], 0), axis=1)
    return (segment, frames - first_frame, indices % FRAME_TOK // GRID_W, indices % GRID_W)


def rope_tables(frame_pos, row_pos, col_pos, head_dim):
    sixth_part = head_dim // 6
    frame_dim = head_dim - 4 * sixth_part
    side_dim = 2 * sixth_part
    frame_freq = 10000.0 ** (-np.arange(0, frame_dim, 2) / frame_dim)
    side_freq = 10000.0 ** (-np.arange(0, side_dim, 2) / side_dim)
    empty_frame = np.zeros(frame_dim // 2)
    empty_side = np.zeros(sixth_part)
    along_frame = jnp.asarray(np.concatenate([frame_freq, empty_side, empty_side]), jnp.float32)
    along_rows = jnp.asarray(np.concatenate([empty_frame, side_freq, empty_side]), jnp.float32)
    along_cols = jnp.asarray(np.concatenate([empty_frame, empty_side, side_freq]), jnp.float32)
    angles = (
        frame_pos.astype(jnp.float32)[:, None] * along_frame[None, :]
        + row_pos.astype(jnp.float32)[:, None] * along_rows[None, :]
        + col_pos.astype(jnp.float32)[:, None] * along_cols[None, :]
    )
    return (jnp.cos(angles), jnp.sin(angles))


def apply_rotary(values, cosine, sine):
    shaped = values.reshape(values.shape[0], values.shape[1], -1, 2)
    first_part = shaped[..., 0]
    second_part = shaped[..., 1]
    cos_wide = cosine[:, None, :]
    sin_wide = sine[:, None, :]
    turned = jnp.stack(
        [
            first_part * cos_wide - second_part * sin_wide,
            first_part * sin_wide + second_part * cos_wide,
        ],
        axis=-1,
    )
    return turned.reshape(values.shape)


def modulate(latents, modulation, segment):
    floats = latents.astype(jnp.float32)
    average = jnp.mean(floats, axis=1, keepdims=True)
    centred = floats - average
    variance = jnp.mean(centred * centred, axis=1, keepdims=True)
    normed = centred * lax.rsqrt(variance + 1e-06)
    chosen = (segment[:, None] == jnp.arange(NSEG, dtype=jnp.int32)[None, :]).astype(jnp.float32)
    shifts = jnp.dot(chosen, modulation[:, 0, :], precision=lax.Precision.HIGHEST)
    scales = jnp.dot(chosen, modulation[:, 1, :], precision=lax.Precision.HIGHEST)
    return (normed * (1.0 + scales) + shifts).astype(jnp.bfloat16)


def attend_block(state, key_block, key_segs, queries, query_seg):
    maxima, totals, accum = state
    heads = queries.shape[1]
    keys_three = key_block[0].reshape(-1, heads, HD)
    values_three = key_block[1].reshape(-1, heads, HD)
    scores = jnp.einsum("qhd,khd->hqk", queries, keys_three, preferred_element_type=jnp.float32) * (
        1.0 / math.sqrt(HD)
    )
    allowed = query_seg[None, :, None] == key_segs[None, None, :]
    newest = jnp.maximum(maxima, jnp.max(jnp.where(allowed, scores, mask_floor), axis=2))
    weights = jnp.where(allowed, jnp.exp(scores - newest[:, :, None]), 0.0)
    factor = jnp.exp(maxima - newest)
    totals = totals * factor + jnp.sum(weights, axis=2)
    product = jnp.einsum(
        "hqk,khd->qhd",
        weights.astype(jnp.bfloat16),
        values_three,
        preferred_element_type=jnp.float32,
    )
    accum = accum * jnp.transpose(factor)[:, :, None] + product
    return (newest, totals, accum)


def attend_piece(state, pieces, key_seg, queries, query_seg):
    count_rows = pieces.shape[1]
    span_rows = math.gcd(count_rows, 512)

    def guarded(carried, key_block, key_segs):
        touches = jnp.logical_and(
            jnp.max(key_segs) >= query_seg[0],
            jnp.min(jnp.where(key_segs >= 0, key_segs, NSEG)) <= query_seg[-1],
        )
        return lax.cond(
            touches,
            lambda inner: attend_block(inner, key_block, key_segs, queries, query_seg),
            lambda inner: inner,
            carried,
        )

    def advance(position, carried):
        key_block = lax.dynamic_slice_in_dim(pieces, position * span_rows, span_rows, 1)
        key_segs = lax.dynamic_slice_in_dim(key_seg, position * span_rows, span_rows, 0)
        return guarded(carried, key_block, key_segs)

    return lax.fori_loop(0, count_rows // span_rows, advance, state)


def body(latents, modulation, w_qkv, qk_gains, frame_counts):
    rows = latents.shape[0]
    model_width = latents.shape[1]
    width_dev = w_qkv.shape[2]
    heads = width_dev // HD
    me_seq = lax.axis_index("seq")
    row_ids = jnp.arange(rows, dtype=jnp.int32)
    indices = me_seq * rows + row_ids
    segment, frame_pos, row_pos, col_pos = token_layout(indices, frame_counts)
    modulated = modulate(latents, modulation, segment)
    projected = jnp.dot(
        modulated, w_qkv.reshape(model_width, 3 * width_dev), preferred_element_type=jnp.float32
    )
    q_raw = projected[:, :width_dev]
    k_raw = projected[:, width_dev : 2 * width_dev]
    values = projected[:, 2 * width_dev :].astype(jnp.bfloat16)
    partial_sums = jnp.stack([jnp.sum(q_raw * q_raw, axis=1), jnp.sum(k_raw * k_raw, axis=1)])
    squares = lax.psum(partial_sums, "mp")
    channels = width_dev * lax.axis_size("mp")
    q_norm = q_raw * lax.rsqrt(squares[0] / channels + 1e-06)[:, None] * qk_gains[0][None, :]
    k_norm = k_raw * lax.rsqrt(squares[1] / channels + 1e-06)[:, None] * qk_gains[1][None, :]
    cosine, sine = rope_tables(frame_pos, row_pos, col_pos, HD)
    queries = apply_rotary(q_norm.reshape(rows, heads, HD), cosine, sine).astype(jnp.bfloat16)
    keys = apply_rotary(k_norm.reshape(rows, heads, HD), cosine, sine).astype(jnp.bfloat16)
    stacked = jnp.stack([keys.reshape(rows, width_dev), values])
    initial = (
        jnp.full((heads, rows), mask_floor, jnp.float32),
        jnp.zeros((heads, rows), jnp.float32),
        jnp.zeros((rows, heads, HD), jnp.float32),
    )
    piece = lax.all_gather(stacked, "seq", axis=1, tiled=True)
    key_index = jnp.arange(piece.shape[1], dtype=jnp.int32)
    key_seg = token_layout(key_index, frame_counts)[0]
    state = attend_piece(initial, piece, key_seg, queries, segment)
    maxima, totals, accum = state
    result = accum / jnp.transpose(totals)[:, :, None]
    return result.astype(jnp.bfloat16).reshape(rows, width_dev)


SLOTS = 8
CHUNKS = 4


def rotary_constants(positions):
    sixth_part = HD // 6
    frame_dim = HD - 4 * sixth_part
    side_dim = 2 * sixth_part
    frame_freq = 10000.0 ** (-np.arange(0, frame_dim, 2) / frame_dim)
    side_freq = 10000.0 ** (-np.arange(0, side_dim, 2) / side_dim)
    token = np.arange(FRAME_TOK)
    angles = np.zeros((FRAME_TOK, HD // 2))
    angles[:, frame_dim // 2 : frame_dim // 2 + sixth_part] = (token // GRID_W)[:, None] * side_freq
    angles[:, frame_dim // 2 + sixth_part :] = (token % GRID_W)[:, None] * side_freq
    wide = np.repeat(angles, 2, axis=1)
    lane = np.arange(HD)
    even = (lane % 2 == 0)[None, :]
    side = (lane >= frame_dim)[None, :]
    tables = np.stack(
        [
            np.where(side, np.cos(wide), 0.0),
            np.where(side & even, -np.sin(wide), 0.0),
            np.where(side & ~even, np.sin(wide), 0.0),
        ]
    )
    turns = np.arange(positions)[:, None] * np.repeat(frame_freq, 2)
    turns = np.pad(turns, ((0, 0), (0, HD - frame_dim)))
    rows = np.stack(
        [
            np.where(side, 0.0, np.cos(turns)),
            np.where(even, -np.sin(turns), 0.0),
            np.where(even, 0.0, np.sin(turns)),
        ],
        axis=1,
    )
    return tables.astype(np.float32), rows.astype(np.float32)


def fused_kernel(
    counts_ref, x_hbm, w_hbm, mod_ref, gain_ref, side_ref, table_ref, out_ref,
    bias_ref, frame_ref, xbuf, ybuf, wbuf, kvg, qbuf, acc, rows_mod, squares, rkeys, maxima, totals, accum,
    xsem, wsem, fsem, ssem, rsem, qs_sem, qr_sem, ks_sem, kr_sem,
):
    rows, width = xbuf.shape
    heads = qbuf.shape[1] // HD
    chunk = width // CHUNKS
    me = lax.axis_index("seq")
    me_mp = lax.axis_index("mp")
    n_mp = squares.shape[1]
    channels = heads * HD * n_mp
    frames = rows // FRAME_TOK

    def peer(rel):
        target = me
        for bit in (1, 2, 4):
            if rel & bit:
                target = target + bit - 2 * bit * (me // bit % 2)
        return {"seq": target}

    def peer_mp(rel):
        return {"mp": (me_mp + rel) % n_mp}

    def x_copy(f):
        span = pl.ds(f * FRAME_TOK, FRAME_TOK)
        return pltpu.make_async_copy(x_hbm.at[span], xbuf.at[span], xsem.at[f])

    def w_copy(which, j):
        span = pl.ds(pl.multiple_of(j * chunk, chunk), chunk)
        return pltpu.make_async_copy(
            w_hbm.at[which, span], wbuf.at[which, span], wsem.at[which, j]
        )

    x_copy(0).start()
    for j in range(CHUNKS):
        w_copy(1, j).start()

    barrier = pltpu.get_barrier_semaphore()
    for rel in range(1, SLOTS):
        pl.semaphore_signal(barrier, inc=1, device_id=peer(rel), device_id_type=pl.DeviceIdType.MESH)
    for rel in range(1, n_mp):
        pl.semaphore_signal(barrier, inc=1, device_id=peer_mp(rel), device_id_type=pl.DeviceIdType.MESH)

    ends, starts = [], []
    for s in range(NSEG):
        starts.append(ends[-1] if s else jnp.int32(0))
        ends.append(starts[-1] + counts_ref[s])

    def segment_of(frame):
        return sum(jnp.where(frame >= end, 1, 0) for end in ends)

    own_seg = [segment_of(me * frames + f) for f in range(frames)]
    for rel in range(SLOTS):
        for g in range(frames):
            key_seg = segment_of(peer(rel)["seq"] * frames + g)
            for f in range(frames):
                bias_ref[f, rel * frames + g] = jnp.where(own_seg[f] == key_seg, 0.0, mask_floor)

    for f in range(frames):
        chosen_start = sum(jnp.where(own_seg[f] == s, starts[s], 0) for s in range(NSEG))
        frame_ref[f] = table_ref[jnp.clip(me * frames + f - chosen_start, 0, table_ref.shape[0] - 1)]
        pair = mod_ref[jnp.minimum(own_seg[f], NSEG - 1)]
        rows_mod[2 * f] = jnp.broadcast_to(pair[0:1, :], (8, width))
        rows_mod[2 * f + 1] = jnp.broadcast_to(1.0 + pair[1:2, :], (8, width))

    def norm_frame(f):
        x_copy(f).wait()

        block, lanes = 128, 128
        groups = width // lanes
        for i in range(FRAME_TOK // block):
            span = slice(f * FRAME_TOK + i * block, f * FRAME_TOK + (i + 1) * block)

            def load(k):
                return xbuf[span, k * lanes : (k + 1) * lanes].astype(jnp.float32)

            total = load(0)
            for k in range(1, groups):
                total = total + load(k)
            average = jnp.sum(total, axis=1, keepdims=True) * (1.0 / width)
            power = jnp.zeros((block, lanes), jnp.float32)
            for k in range(groups):
                centred = load(k) - average
                power = power + centred * centred
            variance = jnp.sum(power, axis=1, keepdims=True) * (1.0 / width)
            inverse = lax.rsqrt(variance + 1e-06)
            for k in range(groups):
                cols = slice(k * lanes, (k + 1) * lanes)
                normed = ((load(k) - average) * inverse).reshape(block // 8, 8, lanes)
                scaled = normed * rows_mod[2 * f + 1, :, cols] + rows_mod[2 * f, :, cols]
                ybuf[span, cols] = scaled.reshape(block, lanes).astype(jnp.bfloat16)

    def project(which, first, last, wait):
        if wait:
            for j in range(CHUNKS):
                w_copy(which, j).wait()
        acc[first:last, :] = jnp.dot(ybuf[first:last, :], wbuf[which], preferred_element_type=jnp.float32)

    def row_squares(kind):
        total = jnp.zeros((rows, HD), jnp.float32)
        for h in range(heads):
            piece = acc[:, h * HD : (h + 1) * HD]
            total = total + piece * piece
        squares[kind, 0] = lax.dot_general(
            jnp.ones((8, HD), jnp.float32), total, (((1,), (1,)), ((), ())),
            precision=lax.Precision.HIGHEST, preferred_element_type=jnp.float32,
        )

    def rotate(kind, f, h):
        span = slice(f * FRAME_TOK, (f + 1) * FRAME_TOK)
        lanes = slice(h * HD, (h + 1) * HD)
        value = acc[span, lanes] * gain_ref[kind : kind + 1, lanes]
        cosine = side_ref[0] + frame_ref[f, 0:1, :]
        below = side_ref[1] + frame_ref[f, 1:2, :]
        above = side_ref[2] + frame_ref[f, 2:3, :]
        return value * cosine + pltpu.roll(value, HD - 1, 1) * below + pltpu.roll(value, 1, 1) * above

    key_sends = [(f, rel) for f in range(frames) for rel in (2, 4, 1)]
    first_sends = [(0, 1, 4, 4), (0, 1, 2, 2), (0, 1, 1, 1)]
    later_sends = [
        (2, 0, 4, 6), (4, 1, 2, 6),
        (2, 0, 1, 3), (2, 1, 1, 3), (4, 0, 1, 5), (4, 1, 1, 5),
        (6, 0, 1, 7), (6, 1, 1, 7),
    ]
    sends = first_sends + later_sends

    def send(entry):
        source, part, rel, landing = entry
        return pltpu.make_async_remote_copy(
            src_ref=kvg.at[source, part], dst_ref=kvg.at[landing, part],
            send_sem=ssem.at[sends.index(entry)], recv_sem=rsem.at[landing, part],
            device_id=peer(rel), device_id_type=pl.DeviceIdType.MESH,
        )

    def send_keys(f, rel):
        span = pl.ds(f * FRAME_TOK, FRAME_TOK)
        return pltpu.make_async_remote_copy(
            src_ref=kvg.at[0, 0, span], dst_ref=kvg.at[rel, 0, span],
            send_sem=fsem.at[key_sends.index((f, rel))], recv_sem=rsem.at[rel, 0],
            device_id=peer(rel), device_id_type=pl.DeviceIdType.MESH,
        )

    def arrived(slot, part):
        pltpu.make_async_copy(kvg.at[slot, part], kvg.at[slot, part], rsem.at[slot, part]).wait()

    def send_squares(kind, rel):
        return pltpu.make_async_remote_copy(
            src_ref=squares.at[kind, 0], dst_ref=squares.at[kind, rel],
            send_sem=qs_sem.at[kind, rel], recv_sem=qr_sem.at[kind, rel],
            device_id=peer_mp(rel), device_id_type=pl.DeviceIdType.MESH,
        )

    def send_rkeys(rel):
        return pltpu.make_async_remote_copy(
            src_ref=rkeys.at[0], dst_ref=rkeys.at[rel],
            send_sem=ks_sem.at[rel], recv_sem=kr_sem.at[rel],
            device_id=peer(rel), device_id_type=pl.DeviceIdType.MESH,
        )

    def inverse_rms(kind):
        total = squares[kind, 0]
        for rel in range(1, n_mp):
            send_squares(kind, rel).wait_recv()
            total = total + squares[kind, rel]
        return lax.rsqrt(total * (1.0 / channels) + 1e-06)

    for f in range(frames):
        norm_frame(f)
        if f == 0:
            for j in range(CHUNKS):
                w_copy(1, j).wait()
            for later in range(1, frames):
                x_copy(later).start()
            for which in (2, 0):
                for j in range(CHUNKS):
                    w_copy(which, j).start()
        project(1, f * FRAME_TOK, (f + 1) * FRAME_TOK, False)
        for h in range(heads):
            kvg[0, 0, f * FRAME_TOK : (f + 1) * FRAME_TOK, h * HD : (h + 1) * HD] = rotate(1, f, h).astype(jnp.bfloat16)
        if f == 0:
            pl.semaphore_wait(barrier, SLOTS - 1 + n_mp - 1)
        for rel in (2, 4, 1):
            send_keys(f, rel).start()
    row_squares(1)
    for rel in range(1, n_mp):
        send_squares(1, rel).start()

    project(2, 0, rows, True)
    kvg[0, 1] = acc[...].astype(jnp.bfloat16)
    for entry in first_sends:
        send(entry).start()
    rkeys[0] = inverse_rms(1) * (math.log2(math.e) / math.sqrt(HD))
    for rel in range(1, SLOTS):
        send_rkeys(rel).start()

    project(0, 0, rows, True)
    row_squares(0)
    for rel in range(1, n_mp):
        send_squares(0, rel).start()
    for f in range(frames):
        for h in range(heads):
            accum[f * FRAME_TOK : (f + 1) * FRAME_TOK, h * HD : (h + 1) * HD] = rotate(0, f, h)

    arrived(2, 0)
    send(later_sends[0]).start()
    send(later_sends[2]).start()
    arrived(4, 0)
    send(later_sends[4]).start()

    rquery = inverse_rms(0)
    column = jnp.transpose(jnp.broadcast_to(rquery[0:1, :], (HD, rows)))
    for h in range(heads):
        lanes = slice(h * HD, (h + 1) * HD)
        qbuf[:, lanes] = (accum[:, lanes] * column).astype(jnp.bfloat16)

    maxima[...] = jnp.full(maxima.shape, mask_floor, jnp.float32)
    totals[...] = jnp.zeros(totals.shape, jnp.float32)
    accum[...] = jnp.zeros(accum.shape, jnp.float32)

    def wait_slot(slot):
        arrived(slot, 0)
        arrived(slot, 1)

    def wait_scale(slot):
        pltpu.make_async_copy(rkeys.at[slot], rkeys.at[slot], kr_sem.at[slot]).wait()

    def attend_slots(pair, carry):
        first, second = 2 * pair, 2 * pair + 1

        @pl.when(pair > 0)
        def _():
            wait_scale(first)

        wait_scale(second)

        @pl.when(pair == 1)
        def _():
            arrived(4, 1)
            send(later_sends[1]).start()
            send(later_sends[5]).start()
            arrived(2, 1)
            send(later_sends[3]).start()

        @pl.when(pair == 3)
        def _():
            arrived(6, 0)
            send(later_sends[6]).start()
            arrived(6, 1)
            send(later_sends[7]).start()

        wait_slot(second)

        def attend_frame(f, inner):
            span = pl.ds(pl.multiple_of(f * FRAME_TOK, FRAME_TOK), FRAME_TOK)
            lane = lax.broadcasted_iota(jnp.int32, (1, 2 * rows), 1)
            shift = jnp.full((1, 2 * rows), bias_ref[f, first * frames], jnp.float32)
            for g in range(1, 2 * frames):
                shift = jnp.where(lane >= g * FRAME_TOK, bias_ref[f, first * frames + g], shift)
            scale = jnp.concatenate([rkeys[first, 0:1, :], rkeys[second, 0:1, :]], axis=1)

            def score(h):
                lanes = slice(h * HD, (h + 1) * HD)
                return jnp.concatenate(
                    [
                        lax.dot_general(
                            qbuf[span, lanes], kvg[slot, 0, :, lanes], (((1,), (1,)), ((), ())),
                            preferred_element_type=jnp.float32,
                        )
                        for slot in (first, second)
                    ],
                    axis=1,
                )

            ones = jnp.ones((rows, HD), jnp.bfloat16)
            ahead = score(0)
            for h in range(heads):
                lanes = slice(h * HD, (h + 1) * HD)
                scores = ahead * scale + shift
                if h + 1 < heads:
                    ahead = score(h + 1)
                before = maxima[h, span, :]
                newest = jnp.maximum(before, jnp.max(scores, axis=1, keepdims=True))
                weights = jnp.exp2(scores - newest[:, 0:1]).astype(jnp.bfloat16)
                factor = jnp.exp2(before - newest)
                product = jnp.dot(
                    weights[:, :rows], jnp.concatenate([kvg[first, 1, :, lanes], ones], axis=1),
                    preferred_element_type=jnp.float32,
                ) + jnp.dot(
                    weights[:, rows:], jnp.concatenate([kvg[second, 1, :, lanes], ones], axis=1),
                    preferred_element_type=jnp.float32,
                )
                totals[h, span, :] = totals[h, span, :] * factor + product[:, HD:]
                accum[span, lanes] = accum[span, lanes] * factor + product[:, :HD]
                maxima[h, span, :] = newest
            return inner

        return lax.fori_loop(0, frames, attend_frame, carry)

    lax.fori_loop(0, SLOTS // 2, attend_slots, 0)
    for h in range(heads):
        lanes = slice(h * HD, (h + 1) * HD)
        out_ref[:, lanes] = (accum[:, lanes] / totals[h]).astype(jnp.bfloat16)

    for f, rel in key_sends:
        send_keys(f, rel).wait_send()
    for entry in sends:
        send(entry).wait_send()
    for rel in range(1, n_mp):
        send_squares(0, rel).wait_send()
        send_squares(1, rel).wait_send()
    for rel in range(1, SLOTS):
        send_rkeys(rel).wait_send()


def fused_body(latents, modulation, w_qkv, qk_gains, frame_counts):
    rows, width = latents.shape
    width_dev = w_qkv.shape[2]
    heads = width_dev // HD
    frames = rows // FRAME_TOK
    n_mp = lax.axis_size("mp")
    side, table = rotary_constants(SLOTS * frames)
    weights = jnp.transpose(w_qkv, (1, 0, 2))
    vmem = pl.BlockSpec(memory_space=pltpu.VMEM)
    smem = pl.BlockSpec(memory_space=pltpu.SMEM)
    hbm = pl.BlockSpec(memory_space=pl.ANY)
    dma = pltpu.SemaphoreType.DMA
    flops = 2 * rows * width * 3 * width_dev + 4 * rows * rows * SLOTS * width_dev
    return pl.pallas_call(
        fused_kernel,
        out_shape=jax.ShapeDtypeStruct((rows, width_dev), jnp.bfloat16),
        in_specs=[smem, hbm, hbm, vmem, vmem, vmem, vmem],
        out_specs=vmem,
        scratch_shapes=[
            pltpu.SMEM((frames, SLOTS * frames), jnp.float32),
            pltpu.VMEM((frames, 3, HD), jnp.float32),
            pltpu.VMEM((rows, width), jnp.bfloat16),
            pltpu.VMEM((rows, width), jnp.bfloat16),
            pltpu.VMEM((3, width, width_dev), jnp.bfloat16),
            pltpu.VMEM((SLOTS, 2, rows, width_dev), jnp.bfloat16),
            pltpu.VMEM((rows, width_dev), jnp.bfloat16),
            pltpu.VMEM((rows, width_dev), jnp.float32),
            pltpu.VMEM((2 * frames, 8, width), jnp.float32),
            pltpu.VMEM((2, n_mp, 8, rows), jnp.float32),
            pltpu.VMEM((SLOTS, 8, rows), jnp.float32),
            pltpu.VMEM((heads, rows, HD), jnp.float32),
            pltpu.VMEM((heads, rows, HD), jnp.float32),
            pltpu.VMEM((rows, width_dev), jnp.float32),
            dma((frames,)),
            dma((3, CHUNKS)),
            dma((3 * frames,)),
            dma((11,)),
            dma((SLOTS, 2)),
            dma((2, n_mp)),
            dma((2, n_mp)),
            dma((SLOTS,)),
            dma((SLOTS,)),
        ],
        compiler_params=pltpu.CompilerParams(
            collective_id=0, has_side_effects=True, vmem_limit_bytes=60 * 1024 * 1024
        ),
        cost_estimate=pl.CostEstimate(flops=flops, bytes_accessed=30000000, transcendentals=12000000),
    )(frame_counts, latents, weights, modulation, qk_gains, side, table)


def solution(mesh):
    in_specs = (P("seq", None), P(), P(None, None, "mp"), P(None, "mp"), P())
    out_specs = P("seq", "mp")
    chosen = fused_body if mesh.shape["seq"] == SLOTS else body
    return jax.shard_map(chosen, mesh=mesh, in_specs=in_specs, out_specs=out_specs, check_vma=False)
```
